32 devices in a mesh: af: 4 (over y, x), col: 2 (over core), ta: 4 (over z).
Axes of the slice: x: 2, y: 2, z: 4, core: 2. Of those that a mesh axis runs over, the one named last changes fastest.
Arguments:
- hidden: bfloat16 [4, 2048, 1536], P('af', 'col'), may hold values from -6 to 6
- lengths: int32 [4], P('af'), may hold values from 256 to 2048, as said below
- norm_gain: bfloat16 [1536], P(('af', 'col')), may hold values from 0.5 to 1.5
- gate_proj: bfloat16 [1536, 3072], P(('af', 'col'), 'ta'), may hold values from -0.15625 to 0.15625
- input_proj: bfloat16 [1536, 3072], P(('af', 'col'), 'ta'), may hold values from -0.15625 to 0.15625
- state_proj: bfloat16 [1536, 256], P(('af', 'col')), may hold values from -0.15625 to 0.15625
- step_proj: bfloat16 [1536, 48], P(('af', 'col'), 'ta'), may hold values from -0.15625 to 0.15625
- conv_input: float32 [4, 3072], P(None, 'ta'), may hold values from -3 to 3
- conv_input_bias: float32 [3072], P('ta'), may hold values from -3 to 3
- conv_state: float32 [4, 256], replicated, may hold values from -3 to 3
- conv_state_bias: float32 [256], replicated, may hold values from -3 to 3
- step_bias: float32 [48], P('ta'), may hold values from -7 to -3
- decay_log: float32 [48], P('ta'), may hold values from -3 to 1
- skip_gain: float32 [48], P('ta'), may hold values from 0.5 to 1.5
- gated_gain: float32 [3072], P('ta'), may hold values from 0.5 to 1.5
- output_proj: bfloat16 [1536, 3072], P(('af', 'col'), 'ta'), may hold values from -0.109375 to 0.109375
- cotangent: bfloat16 [4, 2048, 1536], P('af', 'col'), may hold values from -6 to 6
Outputs:
- block_out: bfloat16 [4, 2048, 1536], P('af', 'col', 'ta')
- hidden_grad: float32 [4, 2048, 1536], P('af', 'col')
- norm_gain_grad: float32 [1536], P(('af', 'col'))
- gate_proj_grad: float32 [1536, 3072], P(('af', 'col'), 'ta')
- input_proj_grad: float32 [1536, 3072], P(('af', 'col'), 'ta')
- state_proj_grad: float32 [1536, 256], P(('af', 'col'))
- step_proj_grad: float32 [1536, 48], P(('af', 'col'), 'ta')
- conv_input_grad: float32 [4, 3072], P(None, 'ta')
- conv_input_bias_grad: float32 [3072], P('ta')
- conv_state_grad: float32 [4, 256], replicated
- conv_state_bias_grad: float32 [256], replicated
- step_bias_grad: float32 [48], P('ta')
- decay_log_grad: float32 [48], P('ta')
- skip_gain_grad: float32 [48], P('ta')
- gated_gain_grad: float32 [3072], P('ta')
- output_proj_grad: float32 [1536, 3072], P(('af', 'col'), 'ta')
The draws below stay inside these ranges and needn't reach their ends.
Inputs may be any that keep to these rules, and one draw needn't show every extreme that they name: `lengths`: every sequence has 256 or more tokens; in every draw some sequence has exactly 2048.
All inputs are finite; a program needn't handle non-finite values.
Results may differ from the reference program's by a relative error of at most 0.0095.
The reference program's roundings to bfloat16 on the way count: a program that leaves them out, or rounds other values in their place, can miss the bound.
Values may be sent and summed in bfloat16 or wider, within the bound.
No kernel may reach another device: no remote copies, remote signals or barrier semaphores. Data moves between devices by JAX's collectives and lax.ppermute only.
A program may use at most 128 MiB of HBM per device.

```python
import jax
import jax.numpy as jnp
from jax import lax

D = 1536
HEADS = 48
HEAD_DIM = 64
NST = 128
KC = 4
STRETCH = 256
LEN = 2048
INNER = 3072
NSEQ = 4


def draw_lengths(key, part):
    first_key, second_key = jax.random.split(jax.random.fold_in(key, 11))
    drawn = jax.random.randint(first_key, (NSEQ,), STRETCH, LEN + 1)
    chosen = jax.random.randint(second_key, (), 0, NSEQ)
    return jnp.where(jnp.arange(NSEQ) == chosen, LEN, drawn).astype(jnp.int32)


def steps_of(own_key, shape, cuts, least, high):
    loudness, own = 1.0, jax.random.fold_in(own_key, 6)
    for axis_at, blocks in cuts:
        draws = jnp.exp(jax.random.uniform(jax.random.fold_in(own, axis_at), (blocks,), jnp.float32, least / len(cuts), high / len(cuts)))
        loudness = loudness * jnp.repeat(draws, shape[axis_at] // blocks).reshape([-1 if axis == axis_at else 1 for axis in range(len(shape))])
    return loudness


def noise(own_key, extent, deviation, bound, cuts=(), dtype=jnp.bfloat16):
    entries = jax.random.normal(own_key, extent, jnp.float32) * deviation
    if len(cuts) > 0:
        entries = steps_of(own_key, extent, cuts, -0.22, 0.18) * entries
    return jnp.clip(entries, min=-bound, max=bound).astype(dtype)


def setup_inputs(seed: int = 0) -> dict:
    streams_of = jax.random.split(jax.random.key(seed), 18)
    hidden = noise(streams_of[0], (NSEQ, LEN, D), 1.0, 6.0, ((0, 4), (1, 2)))
    lengths = draw_lengths(jax.random.fold_in(streams_of[17], 71), 0)
    norm_gain = jnp.clip(1.0 + 0.1 * jax.random.normal(streams_of[2], (D,), jnp.float32), 0.5, 1.5).astype(jnp.bfloat16)
    gate_proj = noise(streams_of[3], (D, INNER), D ** -0.5, 0.15625, ((0, 8), (1, 4)))
    input_proj = noise(streams_of[4], (D, INNER), D ** -0.5, 0.15625, ((0, 8), (1, 4)))
    state_proj = noise(streams_of[5], (D, 2 * NST), D ** -0.5, 0.15625, ((0, 8),))
    step_proj = noise(streams_of[6], (D, HEADS), D ** -0.5, 0.15625, ((0, 8), (1, 4)))
    conv_input = noise(streams_of[7], (KC, INNER), KC ** -0.5, 3.0, ((1, 4),), jnp.float32)
    conv_input_bias = noise(streams_of[8], (INNER,), 0.3, 3.0, ((0, 4),), jnp.float32)
    conv_state = noise(streams_of[9], (KC, 2 * NST), KC ** -0.5, 3.0, (), jnp.float32)
    conv_state_bias = noise(streams_of[10], (2 * NST,), 0.3, 3.0, (), jnp.float32)
    step_bias = jnp.clip(-7.0 + 4.0 * jax.random.uniform(streams_of[11], (HEADS,), jnp.float32) ** steps_of(streams_of[11], (HEADS,), ((0, 4),), -0.2, 0.2), -7.0, -3.0)
    decay_log = jnp.clip(-3.0 + 4.0 * jax.random.uniform(streams_of[12], (HEADS,), jnp.float32) ** steps_of(streams_of[12], (HEADS,), ((0, 4),), -0.2, 0.2), -3.0, 1.0)
    skip_gain = jnp.clip(0.5 + 1.0 * jax.random.uniform(streams_of[13], (HEADS,), jnp.float32) ** steps_of(streams_of[13], (HEADS,), ((0, 4),), -0.2, 0.2), 0.5, 1.5)
    gated_gain = jnp.clip(1.0 + 0.1 * jax.random.normal(streams_of[14], (INNER,), jnp.float32), 0.5, 1.5)
    output_proj = noise(streams_of[15], (D, INNER), INNER ** -0.5, 0.109375, ((0, 8), (1, 4)))
    cotangent = noise(streams_of[16], (NSEQ, LEN, D), 1.0, 6.0, ((0, 4), (1, 2)))
    return dict(hidden=hidden, lengths=lengths, norm_gain=norm_gain, gate_proj=gate_proj, input_proj=input_proj, state_proj=state_proj, step_proj=step_proj, conv_input=conv_input, conv_input_bias=conv_input_bias, conv_state=conv_state, conv_state_bias=conv_state_bias, step_bias=step_bias, decay_log=decay_log, skip_gain=skip_gain, gated_gain=gated_gain, output_proj=output_proj, cotangent=cotangent)


EPS = 1e-05
HIGH = lax.Precision.HIGHEST

@jax.custom_vjp
def low(v):
    return lax.optimization_barrier(v.astype(jnp.bfloat16)).astype(jnp.float32)

@jax.custom_vjp
def low_back(v):
    return v

def low_keep(v):
    return (low(v), None)

def low_pass(kept, grad):
    return (grad,)

def back_keep(v):
    return (v, None)

def back_low(kept, grad):
    return (low(grad),)
low.defvjp(low_keep, low_pass)
low_back.defvjp(back_keep, back_low)

def exact_product(left, right):
    return jnp.dot(left, right, precision=HIGH, preferred_element_type=jnp.float32)

def convolve(sequence_rows, tap_weights, tap_bias):
    span = sequence_rows.shape[0]
    padded = jnp.pad(sequence_rows, ((KC - 1, 0), (0, 0)))
    accum = tap_bias[None, :] + jnp.zeros_like(sequence_rows)
    for tap_index in range(KC):
        accum = accum + tap_weights[tap_index][None, :] * padded[tap_index:tap_index + span]
    return accum

def stretch_step(carry_state, pieces):
    inputs, write_vectors, read_vectors, log_rate, step_size = pieces
    cumulative = jnp.cumsum(log_rate, axis=0)
    scores = jnp.dot(read_vectors, write_vectors.T, precision=HIGH)
    gaps = cumulative[:, None, :] - cumulative[None, :, :]
    stretch_len = log_rate.shape[0]
    causal = jnp.arange(stretch_len)[:, None] >= jnp.arange(stretch_len)[None, :]
    decays = jnp.exp(jnp.where(causal[:, :, None], gaps, -1e+30))
    mixing = scores[:, :, None] * decays * step_size[None, :, :]
    within = jnp.einsum('tsh,shp->thp', mixing, inputs, precision=HIGH)
    carried = jnp.exp(cumulative)[:, :, None] * jnp.einsum('tn,hpn->thp', read_vectors, carry_state, precision=HIGH)
    stretch_end = cumulative[-1]
    weights_tail = jnp.exp(stretch_end[None, :] - cumulative) * step_size
    fresh_state = jnp.einsum('sh,shp,sn->hpn', weights_tail, inputs, write_vectors, precision=HIGH)
    return (jnp.exp(stretch_end)[:, None, None] * carry_state + fresh_state, within + carried)

def block_one(seq_hidden, length, params):
    norm_gain, gate_proj, input_proj, state_proj, step_proj, conv_input, conv_input_bias, conv_state, conv_state_bias, step_bias, decay_log, skip_gain, gated_gain, output_proj = params
    span = seq_hidden.shape[0]
    inverse = lax.rsqrt(lax.optimization_barrier(jnp.mean(seq_hidden * seq_hidden, axis=-1, keepdims=True)) + EPS)
    normed = low(seq_hidden * inverse * norm_gain)
    gate_pre = low_back(exact_product(normed, gate_proj))
    input_pre = low_back(low(exact_product(normed, input_proj)))
    state_pre = low_back(low(exact_product(normed, state_proj)))
    step_raw = low_back(exact_product(normed, step_proj))
    inputs = low(jax.nn.silu(convolve(input_pre, conv_input, conv_input_bias)))
    state_act = jax.nn.silu(convolve(state_pre, conv_state, conv_state_bias))
    write_vectors = low(state_act[:, :NST])
    read_vectors = low(state_act[:, NST:])
    step_size = jax.nn.softplus(step_raw + step_bias)
    log_rate = -jnp.exp(decay_log) * step_size
    blocks = span // STRETCH
    pieces = (inputs.reshape(blocks, STRETCH, HEADS, HEAD_DIM), write_vectors.reshape(blocks, STRETCH, NST), read_vectors.reshape(blocks, STRETCH, NST), log_rate.reshape(blocks, STRETCH, HEADS), step_size.reshape(blocks, STRETCH, HEADS))
    initial = jnp.zeros((HEADS, HEAD_DIM, NST), jnp.float32)
    _, outputs = lax.scan(jax.checkpoint(stretch_step), initial, pieces)
    mixed = outputs.reshape(span, HEADS, HEAD_DIM) + skip_gain[:, None] * inputs.reshape(span, HEADS, HEAD_DIM)
    mixed = low_back(mixed.reshape(span, INNER))
    gated = mixed * jax.nn.silu(gate_pre)
    gate_scale = lax.rsqrt(lax.optimization_barrier(jnp.mean(gated * gated, axis=-1, keepdims=True)) + EPS)
    normal_rows = low(gated * gate_scale * gated_gain)
    mixer_out = exact_product(normal_rows, output_proj.T)
    valid_mask = (jnp.arange(span) < length).astype(jnp.float32)[:, None]
    return seq_hidden + mixer_out * valid_mask

def reference(hidden, lengths, norm_gain, gate_proj, input_proj, state_proj, step_proj, conv_input, conv_input_bias, conv_state, conv_state_bias, step_bias, decay_log, skip_gain, gated_gain, output_proj, cotangent):
    params = (norm_gain.astype(jnp.float32), gate_proj.astype(jnp.float32), input_proj.astype(jnp.float32), state_proj.astype(jnp.float32), step_proj.astype(jnp.float32), conv_input.astype(jnp.float32), conv_input_bias.astype(jnp.float32), conv_state.astype(jnp.float32), conv_state_bias.astype(jnp.float32), step_bias.astype(jnp.float32), decay_log.astype(jnp.float32), skip_gain.astype(jnp.float32), gated_gain.astype(jnp.float32), output_proj.astype(jnp.float32))

    def forward(whole_hidden, weights):

        def one_sequence(seq_items):
            return jax.checkpoint(block_one)(seq_items[0], seq_items[1], weights)
        return lax.map(one_sequence, (whole_hidden, lengths))
    result, pullback = jax.vjp(forward, hidden.astype(jnp.float32), params)
    hidden_grad, weight_grads = pullback(cotangent.astype(jnp.float32))
    return (result.astype(jnp.bfloat16), hidden_grad, weight_grads[0], weight_grads[1], weight_grads[2], weight_grads[3], weight_grads[4], weight_grads[5], weight_grads[6], weight_grads[7], weight_grads[8], weight_grads[9], weight_grads[10], weight_grads[11], weight_grads[12], weight_grads[13])
```

```python
import functools

import jax
import jax.numpy as jnp
from jax import lax
from jax.experimental import pallas as pl
from jax.experimental.pallas import tpu as pltpu
from jax.sharding import PartitionSpec as P

EPS = 1e-05
TB = 128
LANES = 128
SLOT = 16
F32 = jnp.float32
BF16 = jnp.bfloat16


def bit_pairs(axis, bit):
    count = lax.axis_size(axis)
    return [(i, i ^ (1 << bit)) for i in range(count)]


def swap_bit(value, axis, bit):
    return lax.ppermute(value, axis, bit_pairs(axis, bit))


def own_bit(axis, bit):
    return (lax.axis_index(axis) >> bit) & 1


def bits_of(axis):
    return lax.axis_size(axis).bit_length() - 1


def shifted_by(value, axis, steps):
    count = lax.axis_size(axis)
    return lax.ppermute(
        value, axis, [(i, i + steps) for i in range(count) if 0 <= i + steps < count]
    )


def pick(value, index, axis):
    return lax.dynamic_index_in_dim(value, index, axis, False)


def spread_bits(block, axis, order):
    bits = bits_of(axis)
    value = block.reshape((1,) * bits + block.shape)
    for bit in order:
        other = swap_bit(value, axis, bit)
        mine = own_bit(axis, bit)
        dim = bits - 1 - bit
        value = jnp.where(
            mine == 0,
            jnp.concatenate([value, other], axis=dim),
            jnp.concatenate([other, value], axis=dim),
        )
    return value


def gather_rows(local):
    rows, width = local.shape
    half = rows // 2
    order = list(range(bits_of("af")))
    count = lax.axis_size("af")
    first = spread_bits(local[:half], "af", order).reshape(count, half, width)
    second = spread_bits(local[half:], "af", order[::-1]).reshape(count, half, width)
    mine = jnp.stack([first, second], axis=1)
    other = swap_bit(mine, "col", 0)
    place = lax.axis_index("col")
    both = jnp.where(place == 0, jnp.stack([mine, other], 1), jnp.stack([other, mine], 1))
    return both.reshape(count * 2 * rows, width)


def fold_bits(value, axis, order):
    bits = bits_of(axis)
    for bit in order:
        dim = bits - 1 - bit
        mine = own_bit(axis, bit)
        sent = lax.dynamic_slice_in_dim(value, 1 - mine, 1, dim).astype(BF16)
        kept = lax.dynamic_slice_in_dim(value, mine, 1, dim)
        value = kept.astype(F32) + swap_bit(sent, axis, bit).astype(F32)
    return value.reshape(value.shape[bits:])


def scatter_rows(whole):
    count = lax.axis_size("af")
    bits = bits_of("af")
    width = whole.shape[1]
    rows = whole.shape[0] // (2 * count)
    half = rows // 2
    place = lax.axis_index("col")
    blocks = whole.reshape(count, 2, rows, width)
    got = swap_bit(pick(blocks, 1 - place, 1).astype(BF16), "col", 0)
    summed = pick(blocks, place, 1).astype(F32) + got.astype(F32)
    order = list(range(bits))
    lead = (2,) * bits
    first = fold_bits(summed[:, :half].reshape(lead + (half, width)), "af", order)
    second = fold_bits(summed[:, half:].reshape(lead + (half, width)), "af", order[::-1])
    return jnp.concatenate([first, second], axis=0)


def sum_over(value, axis):
    for bit in range(bits_of(axis)):
        value = value + swap_bit(value, axis, bit)
    return value


def chain_sum(part, axis, chunks):
    count = lax.axis_size(axis)
    place = lax.axis_index(axis)
    rows = part.shape[0] // chunks

    def one_way(step, rank):
        got, arrived = None, []
        for tick in range(chunks + count - 2):
            index = jnp.clip(tick - rank, 0, chunks - 1)
            sent = lax.dynamic_slice_in_dim(part, index * rows, rows, 0)
            if got is not None:
                sent = (sent.astype(F32) + got.astype(F32)).astype(BF16)
            got = shifted_by(sent, axis, step)
            arrived.append(got)
        joined = jnp.concatenate(arrived, axis=0)
        return lax.dynamic_slice_in_dim(
            joined, jnp.maximum(rank - 1, 0) * rows, chunks * rows, 0
        )

    return one_way(1, place), one_way(-1, count - 1 - place)


def chain_scatter(part, axis):
    count = lax.axis_size(axis)
    place = lax.axis_index(axis)
    width = part.shape[1] // count

    def block(index):
        return lax.dynamic_slice_in_dim(
            part, jnp.clip(index, 0, count - 1) * width, width, 1
        ).astype(F32)

    def one_way(step, rank, of):
        got = None
        for tick in range(count - 1):
            sent = block(of(count - 1 - tick + rank))
            if got is not None:
                sent = sent + got.astype(F32)
            got = shifted_by(sent.astype(BF16), axis, step)
        return got.astype(F32)

    right = one_way(1, place, lambda b: b)
    left = one_way(-1, count - 1 - place, lambda b: count - 1 - b)
    return block(place) + right + left


def dot(a, b):
    return jnp.dot(a, b, preferred_element_type=F32)


def dot_t(a, b):
    return lax.dot_general(a, b, (((1,), (1,)), ((), ())), preferred_element_type=F32)


def dot_c0(a, b):
    return lax.dot_general(a, b, (((0,), (0,)), ((), ())), preferred_element_type=F32)


def split3(v):
    high = v.astype(BF16).astype(F32)
    rest = v - high
    middle = rest.astype(BF16).astype(F32)
    low = rest - middle
    return (high + pltpu.roll(middle, SLOT, 1) + pltpu.roll(low, 2 * SLOT, 1)).astype(BF16)


def join3(v):
    return v + pltpu.roll(v, LANES - SLOT, 1) + pltpu.roll(v, LANES - 2 * SLOT, 1)


def head_lanes(v, heads):
    lane = lax.broadcasted_iota(jnp.int32, v.shape, 1)
    return jnp.where(lane < heads, v, 0.0)


def reduce_heads(v, e3_ref):
    e1 = e3_ref[0:SLOT, :]
    high = v.astype(BF16)
    low = (v - high.astype(F32)).astype(BF16)
    out = dot_t(high, e1) + dot_t(low, e1)
    return jnp.concatenate(
        [out, jnp.zeros((v.shape[0], LANES - SLOT), F32)], axis=1
    )


def tri(upper):
    row = lax.broadcasted_iota(jnp.int32, (TB, TB), 0)
    col = lax.broadcasted_iota(jnp.int32, (TB, TB), 1)
    return (row <= col) if upper else (row >= col)


def rows8(v):
    out = v[0:8]
    for k in range(8, v.shape[0], 8):
        out = out + v[k : k + 8]
    return out


def low_lanes():
    return lax.broadcasted_iota(jnp.int32, (TB, LANES), 1) < 64


def cut_pair(v, low):
    zero = jnp.zeros_like(v)
    return jnp.concatenate([jnp.where(low, v, zero), jnp.where(low, zero, v)], axis=0)


def forward_states_kernel(
    heads, width, pre_ref, halo_ref, taps_ref, head_ref, e3_ref,
    xp_ref, xbc_ref, slope_ref, dt_ref, state_ref, final_ref, decay_ref,
    pad, state, total,
):
    b = pl.program_id(0)
    conv = xp_ref.shape[1]

    @pl.when(b == 0)
    def _():
        pad[0:8, :] = halo_ref[:, 0:conv].astype(BF16).astype(F32)
        state[...] = jnp.zeros_like(state)
        total[...] = jnp.zeros_like(total)

    @pl.when(b > 0)
    def _():
        pad[0:8, :] = pad[TB : TB + 8, :]

    shifted = pre_ref[:, conv : conv + LANES] + head_ref[0:1, :]
    dt = head_lanes(jax.nn.softplus(shifted), heads)
    la = dt * head_ref[1:2, :]
    cum = head_lanes(join3(dot(tri(False).astype(F32).astype(BF16), split3(la))), heads)
    last = cum[TB - 1 : TB, :]
    dt_ref[:, 0:LANES] = dt
    dt_ref[:, LANES : 2 * LANES] = cum
    dt_ref[:, 2 * LANES : 3 * LANES] = jax.nn.sigmoid(shifted)
    weight = split3(head_lanes(jnp.exp(last - cum) * dt, heads))
    row = lax.broadcasted_iota(jnp.int32, (8, LANES), 0)
    edges = jnp.where(row == 0, jnp.exp(total[...]), jnp.exp(jnp.broadcast_to(last, (8, LANES))))
    edges = dot(split3(head_lanes(edges, heads)), e3_ref[...])
    decay_ref[...] = edges
    total[...] = total[...] + last

    for j in range(0, conv, LANES):
        xb = pre_ref[:, j : j + LANES].astype(BF16)
        xp_ref[:, j : j + LANES] = xb
        pad[8 : 8 + TB, j : j + LANES] = xb.astype(F32)
    for j in list(range(width, conv, LANES)) + list(range(0, width, LANES)):
        xa = jnp.broadcast_to(taps_ref[4:5, j : j + LANES], (TB, LANES))
        for k in range(4):
            xa = xa + taps_ref[k : k + 1, j : j + LANES] * pad[5 + k : 5 + k + TB, j : j + LANES]
        sig = jax.nn.sigmoid(xa)
        act = (xa * sig).astype(BF16)
        xbc_ref[:, j : j + LANES] = act
        slope_ref[:, j : j + LANES] = (sig * (1.0 + xa * (1.0 - sig))).astype(BF16)
        if j < width:
            entering = state[:, j : j + LANES]
            state_ref[:, j : j + LANES] = entering
            wx = (dot(weight, e3_ref[:, j : j + LANES]) * act.astype(F32)).astype(BF16)
            fresh = dot_c0(xbc_ref[:, width : width + LANES], wx)
            leaving = edges[1:2, j : j + LANES] * entering + fresh
            state[:, j : j + LANES] = leaving
            final_ref[:, j : j + LANES] = leaving


def forward_states(pre, halo, taps, head, e3, heads, width):
    rows, full = pre.shape
    conv = full - LANES
    blocks = rows // TB
    block = lambda w: pl.BlockSpec((TB, w), lambda b: (b, 0))
    whole = lambda a: pl.BlockSpec(a.shape, lambda b: (0, 0))
    return pl.pallas_call(
        functools.partial(forward_states_kernel, heads, width),
        grid=(blocks,),
        in_specs=[block(full), whole(halo), whole(taps), whole(head), whole(e3)],
        out_specs=[
            block(conv), block(conv), block(conv), block(3 * LANES), block(width),
            pl.BlockSpec((LANES, width), lambda b: (0, 0)),
            pl.BlockSpec((8, width), lambda b: (b, 0)),
        ],
        out_shape=[
            jax.ShapeDtypeStruct((rows, conv), BF16),
            jax.ShapeDtypeStruct((rows, conv), BF16),
            jax.ShapeDtypeStruct((rows, conv), BF16),
            jax.ShapeDtypeStruct((rows, 3 * LANES), F32),
            jax.ShapeDtypeStruct((blocks * LANES, width), F32),
            jax.ShapeDtypeStruct((LANES, width), F32),
            jax.ShapeDtypeStruct((8 * blocks, width), F32),
        ],
        scratch_shapes=[
            pltpu.VMEM((TB + 8, conv), F32),
            pltpu.VMEM((LANES, width), F32),
            pltpu.VMEM((8, LANES), F32),
        ],
        name="forward_states",
    )(pre, halo, taps, head, e3)


def decay_matrix(cum, cum_t, h):
    return jnp.exp(jnp.minimum(cum[:, h : h + 1] - cum_t[h : h + 1, :], 0.0))


def forward_outputs_kernel(
    heads, width, xbc_ref, dt_ref, state_ref, carry_ref, decay_ref, z_ref, dyn_ref,
    chan_ref, e3_ref, y_ref, enter_ref, sums_ref,
):
    write = xbc_ref[:, width : width + LANES]
    read = xbc_ref[:, width + LANES : width + 2 * LANES]
    dt = split3(dt_ref[:, 0:LANES])
    cum = dt_ref[:, LANES : 2 * LANES]
    grown = split3(head_lanes(jnp.exp(cum), heads))
    cum_t = cum.T
    scores = jnp.where(tri(False), dot_t(read, write), 0.0)
    low = low_lanes()
    squares = jnp.zeros((TB, LANES), F32)
    inner = jnp.zeros((TB, LANES), F32)
    for j in range(0, width, LANES):
        h = j // 64
        sl = slice(j, j + LANES)
        x = xbc_ref[:, sl].astype(F32)
        xd = (dot(dt, e3_ref[:, sl]) * x).astype(BF16)
        entering = (state_ref[:, sl] + decay_ref[0:1, sl] * carry_ref[:, sl]).astype(BF16)
        enter_ref[:, sl] = entering
        mix = jnp.concatenate(
            [(scores * decay_matrix(cum, cum_t, h + q)).astype(BF16) for q in range(2)], axis=1
        )
        y = dot(mix, cut_pair(xd, low))
        y = y + dot(grown, e3_ref[:, sl]) * dot(read, entering)
        y = y + chan_ref[0:1, sl] * x
        y_ref[:, sl] = y
        z = z_ref[:, sl]
        gated = y * (z * jax.nn.sigmoid(z))
        squares = squares + gated * gated
        inner = inner + dyn_ref[:, sl] * chan_ref[1:2, sl] * gated
    row = lax.broadcasted_iota(jnp.int32, (8, TB), 0)
    sq = jnp.sum(squares.T, axis=0, keepdims=True)
    dots = jnp.sum(inner.T, axis=0, keepdims=True)
    sums_ref[...] = jnp.where(row == 0, sq, jnp.where(row == 1, dots, 0.0))


def forward_outputs(xbc, dt, state, carry, decay, z, dyn, chan, e3, heads, width):
    rows, conv = xbc.shape
    blocks = rows // TB
    block = lambda w: pl.BlockSpec((TB, w), lambda b: (b, 0))
    whole = lambda a: pl.BlockSpec(a.shape, lambda b: (0, 0))
    return pl.pallas_call(
        functools.partial(forward_outputs_kernel, heads, width),
        grid=(blocks,),
        in_specs=[
            block(conv), block(3 * LANES), block(width), whole(carry),
            pl.BlockSpec((8, width), lambda b: (b, 0)), block(width), block(width),
            whole(chan), whole(e3),
        ],
        out_specs=[block(width), block(width), pl.BlockSpec((8, TB), lambda b: (0, b))],
        out_shape=[
            jax.ShapeDtypeStruct((rows, width), F32),
            jax.ShapeDtypeStruct((blocks * LANES, width), BF16),
            jax.ShapeDtypeStruct((8, rows), F32),
        ],
        name="forward_outputs",
    )(xbc, dt, state, carry, decay, z, dyn, chan, e3)


def backward_states_kernel(
    heads, width, total_inner, xbc_ref, dt_ref, y_ref, z_ref, dyn_ref, sums_ref, chan_ref, e3_ref,
    yn_ref, dssd_ref, dz_ref, gain_ref, dstate_ref, dfinal_ref, decay_ref,
    dstate, total,
):
    i = pl.program_id(0)

    @pl.when(i == 0)
    def _():
        dstate[...] = jnp.zeros_like(dstate)
        total[...] = jnp.zeros_like(total)
        gain_ref[...] = jnp.zeros_like(gain_ref)

    read = xbc_ref[:, width + LANES : width + 2 * LANES]
    cum = dt_ref[:, LANES : 2 * LANES]
    last = cum[TB - 1 : TB, :]
    grown = split3(head_lanes(jnp.exp(cum), heads))
    row = lax.broadcasted_iota(jnp.int32, (8, LANES), 0)
    edges = jnp.where(row == 0, jnp.exp(total[...]), jnp.exp(jnp.broadcast_to(last, (8, LANES))))
    edges = dot(split3(head_lanes(edges, heads)), e3_ref[...])
    decay_ref[...] = edges
    total[...] = total[...] + last
    scale_row = lax.rsqrt(sums_ref[0:1, :] / total_inner + EPS)
    inner_row = sums_ref[1:2, :] / total_inner
    scale = jnp.broadcast_to(scale_row, (TB, TB)).T
    inner = jnp.broadcast_to(scale_row * scale_row * scale_row * inner_row, (TB, TB)).T
    for j in range(0, width, LANES):
        sl = slice(j, j + LANES)
        y = y_ref[:, sl]
        z = z_ref[:, sl]
        dyn = dyn_ref[:, sl]
        gain = chan_ref[1:2, sl]
        sig = jax.nn.sigmoid(z)
        act = z * sig
        gated = y * act
        scaled = gated * scale
        yn_ref[:, sl] = (scaled * gain).astype(BF16)
        gain_ref[:, sl] += rows8(dyn * scaled)
        dgated = scale * (dyn * gain) - gated * inner
        dssd = (dgated * act).astype(BF16)
        dssd_ref[:, sl] = dssd
        slope = sig * (1.0 + z * (1.0 - sig))
        dz_ref[:, sl] = (dgated * y * slope).astype(BF16)
        edy = (dot(grown, e3_ref[:, sl]) * dssd.astype(F32)).astype(BF16)
        leaving = dstate[:, sl]
        dstate_ref[:, sl] = leaving
        entering = edges[1:2, sl] * leaving + dot_c0(read, edy)
        dstate[:, sl] = entering
        dfinal_ref[:, sl] = entering


def backward_states(xbc, dt, y, z, dyn, sums, chan, e3, heads, width, total_inner):
    rows, conv = xbc.shape
    blocks = rows // TB
    back = blocks - 1
    block = lambda w: pl.BlockSpec((TB, w), lambda i: (back - i, 0))
    whole = lambda a: pl.BlockSpec(a.shape, lambda i: (0, 0))
    return pl.pallas_call(
        functools.partial(backward_states_kernel, heads, width, float(total_inner)),
        grid=(blocks,),
        in_specs=[
            block(conv), block(3 * LANES), block(width), block(width), block(width),
            pl.BlockSpec((8, TB), lambda i: (0, back - i)), whole(chan), whole(e3),
        ],
        out_specs=[
            block(width), block(width), block(width),
            pl.BlockSpec((8, width), lambda i: (0, 0)),
            block(width),
            pl.BlockSpec((LANES, width), lambda i: (0, 0)),
            pl.BlockSpec((8, width), lambda i: (back - i, 0)),
        ],
        out_shape=[
            jax.ShapeDtypeStruct((rows, width), BF16),
            jax.ShapeDtypeStruct((rows, width), BF16),
            jax.ShapeDtypeStruct((rows, width), BF16),
            jax.ShapeDtypeStruct((8, width), F32),
            jax.ShapeDtypeStruct((blocks * LANES, width), F32),
            jax.ShapeDtypeStruct((LANES, width), F32),
            jax.ShapeDtypeStruct((8 * blocks, width), F32),
        ],
        scratch_shapes=[pltpu.VMEM((LANES, width), F32), pltpu.VMEM((8, LANES), F32)],
        name="backward_states",
    )(xbc, dt, y, z, dyn, sums, chan, e3)


def backward_inputs_kernel(
    heads, width, xbc_ref, xp_ref, slope_ref, dt_ref, y_ref, dssd_ref, enter_ref,
    dstate_ref, dcarry_ref, decay_ref, halo_ref, taps_ref, head_ref, chan_ref, e3_ref,
    dpre_ref, tail_ref, rim_ref, conv_ref, headg_ref, skip_ref,
    pad, rim, grown_dy, weighted_x, dleave,
):
    i = pl.program_id(0)
    conv = xp_ref.shape[1]

    @pl.when(i == 0)
    def _():
        pad[TB : TB + 8, :] = jnp.zeros((8, conv), F32)
        conv_ref[...] = jnp.zeros_like(conv_ref)
        headg_ref[...] = jnp.zeros_like(headg_ref)
        skip_ref[...] = jnp.zeros_like(skip_ref)

    @pl.when(i > 0)
    def _():
        pad[TB : TB + 8, :] = pad[0:8, :]

    write = xbc_ref[:, width : width + LANES]
    read = xbc_ref[:, width + LANES : width + 2 * LANES]
    dt_own = dt_ref[:, 0:LANES]
    cum = dt_ref[:, LANES : 2 * LANES]
    last = cum[TB - 1 : TB, :]
    dt = split3(dt_own)
    grown = split3(head_lanes(jnp.exp(cum), heads))
    fading = split3(head_lanes(jnp.exp(last - cum), heads))
    cum_t = cum.T
    causal = tri(False)
    scores = jnp.where(causal, dot_t(read, write), 0.0)
    low = low_lanes()
    dscores = jnp.zeros((TB, TB), F32)
    e1 = e3_ref[0:SLOT, :]
    dcum = jnp.zeros((TB, SLOT), F32)
    ddt = jnp.zeros((TB, SLOT), F32)
    through = jnp.zeros((8, SLOT), F32)

    def head_sum(v, sl):
        high = v.astype(BF16)
        rest = (v - high.astype(F32)).astype(BF16)
        return dot_t(high, e1[:, sl]) + dot_t(rest, e1[:, sl])

    for j in range(0, width, LANES):
        h = j // 64
        sl = slice(j, j + LANES)
        xb = xbc_ref[:, sl]
        x = xb.astype(F32)
        dyb = dssd_ref[:, sl]
        dy = dyb.astype(F32)
        dt_wide = dot(dt, e3_ref[:, sl])
        fading_wide = dot(fading, e3_ref[:, sl])
        xdb = (dt_wide * x).astype(BF16)
        xd = xdb.astype(F32)
        dy_cut = cut_pair(dyb, low)
        dmix = dot_t(dy_cut, xdb)
        mixes = []
        for q in range(2):
            fade = decay_matrix(cum, cum_t, h + q)
            dscores = dscores + dmix[q * TB : (q + 1) * TB] * fade
            mixes.append((scores * fade).astype(BF16))
        dxd = dot_c0(jnp.concatenate(mixes, axis=0), dy_cut)
        leave = dstate_ref[:, sl] + decay_ref[0:1, sl] * dcarry_ref[:, sl]
        leaveb = leave.astype(BF16)
        dleave[:, sl] = leaveb
        tail = fading_wide * dot(write, leaveb)
        dxd = dxd + tail
        skip = chan_ref[0:1, sl]
        dx = dt_wide * dxd + skip * dy
        pad[0:TB, sl] = dx * slope_ref[:, sl].astype(F32)
        grown_dy[:, sl] = (dot(grown, e3_ref[:, sl]) * dy).astype(BF16)
        weighted_x[:, sl] = (fading_wide * dt_wide * x).astype(BF16)
        dcum = dcum + head_sum(dy * (y_ref[:, sl] - skip * x) - xd * dxd, sl)
        ddt = ddt + head_sum(x * dxd, sl)
        enter = enter_ref[:, sl].astype(F32)
        edge = rows8(xd * tail) + rows8(leave * enter) * decay_ref[1:2, sl]
        through = through + head_sum(edge, sl)
        skip_ref[:, sl] += rows8(dy * x)

    dscores = jnp.where(causal, dscores, 0.0).astype(BF16)
    dread = dot(dscores, write) + dot_t(grown_dy[...], enter_ref[...])
    dwrite = dot_c0(dscores, read) + dot_t(weighted_x[...], dleave[...])
    pad[0:TB, width : width + LANES] = dwrite * slope_ref[:, width : width + LANES].astype(F32)
    pad[0:TB, width + LANES : conv] = dread * slope_ref[:, width + LANES : conv].astype(F32)

    blank = jnp.zeros((TB, LANES - SLOT), F32)
    dcum = jnp.concatenate([dcum, blank], axis=1)
    ddt = jnp.concatenate([ddt, blank], axis=1)
    through = jnp.concatenate([jnp.sum(through, axis=0, keepdims=True), blank[0:1]], axis=1)
    dla = join3(dot(tri(True).astype(F32).astype(BF16), split3(dcum)))
    dla = head_lanes(dla + through, heads)
    ddt = ddt + head_ref[1:2, :] * dla
    du = head_lanes(ddt * dt_ref[:, 2 * LANES : 3 * LANES], heads)
    dpre_ref[:, conv : conv + LANES] = du.astype(BF16)
    headg_ref[0:8, :] += rows8(du)
    headg_ref[8:16, :] += rows8(dla * dt_own)

    for j in range(0, conv, LANES):
        sl = slice(j, j + LANES)
        xp = xp_ref[:, sl].astype(F32)
        dxp = jnp.zeros((TB, LANES), F32)
        for k in range(4):
            piece = pad[3 - k : 3 - k + TB, sl]
            dxp = dxp + taps_ref[k : k + 1, sl] * piece
            conv_ref[8 * k : 8 * k + 8, sl] += rows8(xp * piece)
            if k == 3:
                conv_ref[32:40, sl] += rows8(piece)
        dpre_ref[:, sl] = dxp.astype(BF16)

        @pl.when(i == 0)
        def _():
            tail_ref[:, sl] = dxp[TB - 8 : TB]

    @pl.when(i == pl.num_programs(0) - 1)
    def _():
        rim[0:8, :] = jnp.zeros((8, conv), F32)
        rim[8:16, :] = pad[0:8, :]
        xp = halo_ref[:, 0:conv].astype(BF16).astype(F32)
        out = jnp.zeros((8, conv), F32)
        for k in range(4):
            piece = rim[3 - k : 11 - k, :]
            out = out + taps_ref[k : k + 1, :] * piece
            conv_ref[8 * k : 8 * k + 8, :] += xp * piece
        rim_ref[...] = out


def backward_inputs(
    xbc, xp, slope, dt, y, dssd, enter, dstate, dcarry, decay, halo, taps, head, chan, e3,
    heads, width,
):
    rows, conv = xbc.shape
    blocks = rows // TB
    back = blocks - 1
    block = lambda w: pl.BlockSpec((TB, w), lambda i: (back - i, 0))
    whole = lambda a: pl.BlockSpec(a.shape, lambda i: (0, 0))
    kept = lambda r, w: pl.BlockSpec((r, w), lambda i: (0, 0))
    return pl.pallas_call(
        functools.partial(backward_inputs_kernel, heads, width),
        grid=(blocks,),
        in_specs=[
            block(conv), block(conv), block(conv), block(3 * LANES), block(width), block(width),
            block(width), block(width), whole(dcarry),
            pl.BlockSpec((8, width), lambda i: (back - i, 0)),
            whole(halo), whole(taps), whole(head), whole(chan), whole(e3),
        ],
        out_specs=[
            block(conv + LANES), kept(8, conv), kept(8, conv), kept(40, conv),
            kept(16, LANES), kept(8, width),
        ],
        out_shape=[
            jax.ShapeDtypeStruct((rows, conv + LANES), BF16),
            jax.ShapeDtypeStruct((8, conv), F32),
            jax.ShapeDtypeStruct((8, conv), F32),
            jax.ShapeDtypeStruct((40, conv), F32),
            jax.ShapeDtypeStruct((16, LANES), F32),
            jax.ShapeDtypeStruct((8, width), F32),
        ],
        scratch_shapes=[
            pltpu.VMEM((TB + 8, conv), F32),
            pltpu.VMEM((16, conv), F32),
            pltpu.VMEM((TB, width), BF16),
            pltpu.VMEM((TB, width), BF16),
            pltpu.VMEM((LANES, width), BF16),
        ],
        name="backward_inputs",
    )(
        xbc, xp, slope, dt, y, dssd, enter, dstate, dcarry, decay, halo, taps, head, chan, e3
    )


def outer(left, right):
    return lax.dot_general(left, right, (((0,), (0,)), ((), ())), preferred_element_type=F32)


def against(left, right):
    return lax.dot_general(left, right, (((1,), (1,)), ((), ())), preferred_element_type=F32)


def product(left, right):
    return jnp.dot(left, right, preferred_element_type=F32)


def row_of(values, width):
    return jnp.pad(values.astype(F32), (0, width - values.shape[0]))[None, :]


def body(
    hidden, lengths, norm_gain, gate_proj, input_proj, state_proj, step_proj, conv_input,
    conv_input_bias, conv_state, conv_state_bias, step_bias, decay_log, skip_gain, gated_gain,
    output_proj, cotangent,
):
    _, positions, model = hidden.shape
    heads = step_bias.shape[0]
    width = gated_gain.shape[0]
    both = state_proj.shape[1]
    conv = width + both
    local_rows = norm_gain.shape[0]
    total_inner = width * lax.axis_size("ta")
    h = hidden[0]
    cot = cotangent[0]

    packed = jnp.concatenate(
        [
            input_proj, state_proj, step_proj, norm_gain[:, None],
            jnp.zeros((local_rows, LANES - heads - 1), BF16),
        ],
        axis=1,
    )
    halo_h = shifted_by(h[positions - 8 :], "col", 1)
    packed_full = gather_rows(packed)
    gate_full = gather_rows(gate_proj)
    output_full = gather_rows(output_proj)

    lane = jnp.arange(LANES)
    chosen = jnp.broadcast_to((lane == heads).astype(BF16)[None, :], (8, LANES))
    gain = against(chosen, packed_full[:, conv:])[0:1]

    e3 = (
        (jnp.arange(LANES)[:, None] % SLOT == jnp.arange(width)[None, :] // (width // heads))
        & (jnp.arange(LANES)[:, None] < 3 * SLOT)
    ).astype(BF16)
    taps = jnp.concatenate(
        [
            jnp.concatenate([conv_input, conv_state], axis=1),
            jnp.concatenate([conv_input_bias, conv_state_bias])[None, :],
            jnp.zeros((3, conv), F32),
        ],
        axis=0,
    )
    rate = -jnp.exp(decay_log)
    head = jnp.concatenate(
        [row_of(step_bias, LANES), row_of(rate, LANES), jnp.zeros((6, LANES), F32)], axis=0
    )
    chan = jnp.concatenate(
        [
            jnp.repeat(skip_gain, width // heads)[None, :], gated_gain[None, :],
            jnp.zeros((6, width), F32),
        ],
        axis=0,
    )

    def normalise(rows):
        values = rows.astype(F32)
        inverse = lax.rsqrt(jnp.mean(values * values, axis=-1, keepdims=True) + EPS)
        return inverse, (values * inverse * gain).astype(BF16)

    inverse, normed = normalise(h)
    _, halo_normed = normalise(halo_h)
    pre = product(normed, packed_full)
    halo = product(halo_normed, packed_full)
    xp, xbc, slope, dt, state, final, decay = forward_states(
        pre, halo, taps, head, e3, heads, width
    )
    carry = shifted_by(final, "col", 1)
    z = product(normed, gate_full)

    position = lax.axis_index("col") * positions + jnp.arange(positions)
    valid = (position < lengths[0]).astype(F32)[:, None]
    dmix = (cot.astype(F32) * valid).astype(BF16)
    dyn = product(dmix, output_full)
    y, enter, sums = forward_outputs(xbc, dt, state, carry, decay, z, dyn, chan, e3, heads, width)
    sums = sum_over(sums, "ta")
    yn, dssd, dz, gain_part, dstate, dfinal, fade = backward_states(
        xbc, dt, y, z, dyn, sums, chan, e3, heads, width, total_inner
    )
    dcarry = shifted_by(dfinal, "col", -1)

    mixed = chain_scatter(against(yn, output_full).astype(BF16), "ta")
    quarter = mixed.shape[1]
    own = lax.dynamic_slice_in_dim(h, lax.axis_index("ta") * quarter, quarter, 1).astype(F32)
    block_out = (own + mixed * valid).astype(BF16)

    output_grad = scatter_rows(outer(dmix, yn).astype(BF16))
    gate_grad = scatter_rows(outer(normed, dz).astype(BF16))

    dpre, tail, rim, conv_part, head_part, skip_part = backward_inputs(
        xbc, xp, slope, dt, y, dssd, enter, dstate, dcarry, fade, halo, taps, head, chan, e3,
        heads, width,
    )
    tail = (tail + shifted_by(rim, "col", -1)).astype(BF16)
    dpre = lax.dynamic_update_slice(dpre, tail, (positions - 8, 0))

    partial = (against(dz, gate_full) + against(dpre, packed_full)).astype(BF16)
    packed_grad = scatter_rows(outer(normed, dpre).astype(BF16))
    before, after = chain_sum(partial, "ta", 8)
    dnormed = partial.astype(F32) + before.astype(F32) + after.astype(F32)
    hf = h.astype(F32)
    weighted = dnormed * gain
    inner = jnp.sum(weighted * hf, axis=-1, keepdims=True)
    hidden_grad = cot.astype(F32) + inverse * weighted - hf * inverse**3 * inner / model

    input_grad = packed_grad[:, :width]
    state_grad = packed_grad[:, width:conv]
    step_grad = packed_grad[:, conv : conv + heads]
    rows_dot = (
        jnp.sum(gate_grad * gate_proj.astype(F32), axis=1)
        + jnp.sum(input_grad * input_proj.astype(F32), axis=1)
        + jnp.sum(state_grad * state_proj.astype(F32), axis=1)
        + jnp.sum(step_grad * step_proj.astype(F32), axis=1)
    )

    conv_sums = jnp.sum(conv_part.reshape(5, 8, conv), axis=1)
    head_sums = jnp.sum(head_part.reshape(2, 8, LANES), axis=1)
    small = jnp.concatenate(
        [
            jnp.pad(conv_sums, ((0, 0), (0, LANES * 2))),
            jnp.concatenate(
                [
                    jnp.sum(gain_part, axis=0), jnp.zeros((both,), F32), head_sums[0], head_sums[1],
                ]
            )[None, :],
            jnp.pad(jnp.sum(skip_part, axis=0), (0, both + 2 * LANES))[None, :],
            jnp.zeros((1, conv + 2 * LANES), F32),
        ],
        axis=0,
    )
    small = sum_over(sum_over(small, "col"), "af")
    third = jnp.concatenate(
        [state_grad, jnp.broadcast_to(rows_dot[:, None], (local_rows, LANES))], axis=1
    )
    third = jnp.concatenate([third, jnp.pad(small[:, width:conv], ((0, 0), (0, LANES)))], axis=0)
    third = sum_over(third, "ta")
    state_grad = third[:local_rows, :both]
    norm_gain_grad = third[:local_rows, both] / norm_gain.astype(F32)
    state_small = third[local_rows:, :both]
    skip_grad = jnp.sum(small[6, :width].reshape(heads, width // heads), axis=1)
    return (
        block_out[None],
        hidden_grad[None],
        norm_gain_grad,
        gate_grad,
        input_grad,
        state_grad,
        step_grad,
        small[0:4, :width],
        small[4, :width],
        state_small[0:4],
        state_small[4],
        small[5, conv : conv + heads],
        rate * small[5, conv + LANES : conv + LANES + heads],
        skip_grad,
        small[5, :width],
        output_grad,
    )


def solution(mesh):
    return jax.shard_map(
        body,
        mesh=mesh,
        in_specs=(
            P("af", "col", None),
            P("af"),
            P(("af", "col")),
            P(("af", "col"), "ta"),
            P(("af", "col"), "ta"),
            P(("af", "col"), None),
            P(("af", "col"), "ta"),
            P(None, "ta"),
            P("ta"),
            P(),
            P(),
            P("ta"),
            P("ta"),
            P("ta"),
            P("ta"),
            P(("af", "col"), "ta"),
            P("af", "col", None),
        ),
        out_specs=(
            P("af", "col", "ta"),
            P("af", "col", None),
            P(("af", "col")),
            P(("af", "col"), "ta"),
            P(("af", "col"), "ta"),
            P(("af", "col"), None),
            P(("af", "col"), "ta"),
            P(None, "ta"),
            P("ta"),
            P(),
            P(),
            P("ta"),
            P("ta"),
            P("ta"),
            P("ta"),
            P(("af", "col"), "ta"),
        ),
        check_vma=False,
    )
```

```python
import functools

import jax
import jax.numpy as jnp
from jax import lax
from jax.experimental import pallas as pl
from jax.experimental.pallas import tpu as pltpu
from jax.sharding import PartitionSpec as P


EPS = 1e-05
TB = 128
LANES = 128
SLOT = 16
F32 = jnp.float32
BF16 = jnp.bfloat16


def bit_pairs(axis, bit):
    count = lax.axis_size(axis)
    return [(i, i ^ (1 << bit)) for i in range(count)]


def swap_bit(value, axis, bit):
    return lax.ppermute(value, axis, bit_pairs(axis, bit))


def own_bit(axis, bit):
    return (lax.axis_index(axis) >> bit) & 1


def bits_of(axis):
    return lax.axis_size(axis).bit_length() - 1


def shifted_by(value, axis, steps):
    count = lax.axis_size(axis)
    return lax.ppermute(
        value, axis, [(i, i + steps) for i in range(count) if 0 <= i + steps < count]
    )


def pick(value, index, axis):
    return lax.dynamic_index_in_dim(value, index, axis, False)


def spread_bits(block, axis, order):
    bits = bits_of(axis)
    value = block.reshape((1,) * bits + block.shape)
    for bit in order:
        other = swap_bit(value, axis, bit)
        mine = own_bit(axis, bit)
        dim = bits - 1 - bit
        value = jnp.where(
            mine == 0,
            jnp.concatenate([value, other], axis=dim),
            jnp.concatenate([other, value], axis=dim),
        )
    return value


def place_kernel(splits, where_ref, *refs):
    pieces, outs = refs[:10], refs[10:]
    place = where_ref[1]
    half = pieces[3].shape[0]
    now = pl.program_id(0)
    for which in range(2):
        own, x, y, upper, lower = pieces[5 * which : 5 * which + 5]
        slot = place if which == 0 else 1 - place
        for relative, source in enumerate((own, x, y, None)):

            @pl.when(now == relative)
            def _():
                for (start, stop), out in zip(splits, outs):
                    if source is None:
                        out[pl.ds(slot, 1), 0:half, :] = upper[:, start:stop][None]
                        out[pl.ds(slot, 1), half:, :] = lower[:, start:stop][None]
                    else:
                        out[pl.ds(slot, 1)] = source[:, start:stop][None]


def place_rows(mine, other, widths):
    rows, _ = mine[0].shape
    edges = [sum(widths[:k]) for k in range(len(widths) + 1)]
    where = jnp.stack([lax.axis_index("af"), lax.axis_index("col")]).astype(jnp.int32)
    pieces = list(mine) + list(other)
    outs = pl.pallas_call(
        functools.partial(place_kernel, list(zip(edges[:-1], edges[1:]))),
        grid_spec=pltpu.PrefetchScalarGridSpec(
            num_scalar_prefetch=1,
            grid=(4,),
            in_specs=[pl.BlockSpec(piece.shape, lambda i, at: (0, 0)) for piece in pieces],
            out_specs=[
                pl.BlockSpec((2, rows, w), lambda i, at: (at[0] ^ i, 0, 0)) for w in widths
            ],
        ),
        out_shape=[jax.ShapeDtypeStruct((8, rows, w), mine[0].dtype) for w in widths],
        name="place_rows",
    )(where, *pieces)
    return [out.reshape(8 * rows, out.shape[2]) for out in outs]


def gather_rows(local, widths):
    rows, width = local.shape
    half = rows // 2
    if bits_of("af") == 2:
        x = swap_bit(local, "af", 0)
        y = swap_bit(local, "af", 1)
        upper = swap_bit(x[:half], "af", 1)
        lower = swap_bit(y[half:], "af", 0)
        mine = (local, x, y, upper, lower)
        other = [swap_bit(v, "col", 0) for v in mine]
        return place_rows(mine, other, widths)
    order = list(range(bits_of("af")))
    count = lax.axis_size("af")
    first = spread_bits(local[:half], "af", order).reshape(count, half, width)
    second = spread_bits(local[half:], "af", order[::-1]).reshape(count, half, width)
    mine = jnp.concatenate([first, second], axis=1)
    other = swap_bit(mine, "col", 0)
    place = lax.axis_index("col")
    both = jnp.where(place == 0, jnp.stack([mine, other], 1), jnp.stack([other, mine], 1))
    both = both.reshape(count * 2 * rows, width)
    edges = [sum(widths[:k]) for k in range(len(widths) + 1)]
    return [both[:, i:j] for i, j in zip(edges[:-1], edges[1:])]


def gather_vector(local):
    count = lax.axis_size("af") * 2
    place = lax.axis_index("af") * 2 + lax.axis_index("col")
    own = jnp.arange(count)[:, None] == place
    whole = jnp.where(own, local.astype(F32)[None, :], 0.0).reshape(1, -1)
    return sum_over(sum_over(whole, "af"), "col")


def fold_bits(value, axis, order):
    bits = bits_of(axis)
    for bit in order:
        dim = bits - 1 - bit
        mine = own_bit(axis, bit)
        sent = lax.dynamic_slice_in_dim(value, 1 - mine, 1, dim).astype(BF16)
        kept = lax.dynamic_slice_in_dim(value, mine, 1, dim)
        value = kept.astype(F32) + swap_bit(sent, axis, bit).astype(F32)
    return value.reshape(value.shape[bits:])


def scatter_rows(whole):
    count = lax.axis_size("af")
    bits = bits_of("af")
    width = whole.shape[1]
    rows = whole.shape[0] // (2 * count)
    half = rows // 2
    place = lax.axis_index("col")
    blocks = whole.reshape(count, 2, rows, width)
    got = swap_bit(pick(blocks, 1 - place, 1).astype(BF16), "col", 0)
    summed = pick(blocks, place, 1).astype(F32) + got.astype(F32)
    order = list(range(bits))
    lead = (2,) * bits
    first = fold_bits(summed[:, :half].reshape(lead + (half, width)), "af", order)
    second = fold_bits(summed[:, half:].reshape(lead + (half, width)), "af", order[::-1])
    return jnp.concatenate([first, second], axis=0)


def sum_over(value, axis):
    for bit in range(bits_of(axis)):
        value = value + swap_bit(value, axis, bit)
    return value


def chain_sum_step(part, axis, tick, chunks, got, needed=None):
    count = lax.axis_size(axis)
    place = lax.axis_index(axis)
    rows = part.shape[0] // chunks
    sends, pairs = [], []
    for side, step in enumerate((1, -1)):
        rank = place if step == 1 else count - 1 - place
        senders = [i for i in range(count - 1) if 0 <= tick - i < chunks]
        if len(senders) == 1:
            index = tick - senders[0]
        else:
            index = jnp.clip(tick - rank, 0, chunks - 1)
        sent = lax.dynamic_slice_in_dim(part, index * rows, rows, 0)
        if got is not None:
            sent = (sent.astype(F32) + got[side].astype(F32)).astype(BF16)
        sends.append(sent)
        pairs.append(
            [(i, i + 1) if step == 1 else (count - 1 - i, count - 2 - i) for i in senders]
        )
    extra = () if needed is None else (needed,)
    sends = lax.optimization_barrier(tuple(sends) + extra)[:2]
    out = [lax.ppermute(sends[side], axis, pairs[side]) for side in range(2)]
    return lax.optimization_barrier(tuple(out))


def dot(a, b):
    return jnp.dot(a, b, preferred_element_type=F32)


def dot_t(a, b):
    return lax.dot_general(a, b, (((1,), (1,)), ((), ())), preferred_element_type=F32)


def dot_c0(a, b):
    return lax.dot_general(a, b, (((0,), (0,)), ((), ())), preferred_element_type=F32)


def split3(v):
    high = v.astype(BF16).astype(F32)
    rest = v - high
    middle = rest.astype(BF16).astype(F32)
    low = rest - middle
    return (high + pltpu.roll(middle, SLOT, 1) + pltpu.roll(low, 2 * SLOT, 1)).astype(BF16)


def join3(v):
    return v + pltpu.roll(v, LANES - SLOT, 1) + pltpu.roll(v, LANES - 2 * SLOT, 1)


def head_lanes(v, heads):
    lane = lax.broadcasted_iota(jnp.int32, v.shape, 1)
    return jnp.where(lane < heads, v, 0.0)


def tri(upper):
    row = lax.broadcasted_iota(jnp.int32, (TB, TB), 0)
    col = lax.broadcasted_iota(jnp.int32, (TB, TB), 1)
    return (row <= col) if upper else (row >= col)


def rows8(v):
    out = v[0:8]
    for k in range(8, v.shape[0], 8):
        out = out + v[k : k + 8]
    return out


def low_lanes():
    return lax.broadcasted_iota(jnp.int32, (TB, LANES), 1) < 64


def cut_pair(v, low):
    zero = jnp.zeros_like(v)
    return jnp.concatenate([jnp.where(low, v, zero), jnp.where(low, zero, v)], axis=0)


def forward_states_kernel(
    heads, width, pre_ref, halo_ref, taps_ref, head_ref, e3_ref,
    xp_ref, xbc_ref, slope_ref, dt_ref, state_ref, final_ref, decay_ref,
    pad, state, total,
):
    b = pl.program_id(0)
    conv = xp_ref.shape[1]

    @pl.when(b == 0)
    def _():
        pad[0:8, :] = halo_ref[:, 0:conv].astype(BF16).astype(F32)
        state[...] = jnp.zeros_like(state)
        total[...] = jnp.zeros_like(total)

    @pl.when(b > 0)
    def _():
        pad[0:8, :] = pad[TB : TB + 8, :]

    shifted = pre_ref[:, conv : conv + LANES] + head_ref[0:1, :]
    dt = head_lanes(jax.nn.softplus(shifted), heads)
    la = dt * head_ref[1:2, :]
    cum = head_lanes(join3(dot(tri(False).astype(F32).astype(BF16), split3(la))), heads)
    last = cum[TB - 1 : TB, :]
    dt_ref[:, 0:LANES] = dt
    dt_ref[:, LANES : 2 * LANES] = cum
    dt_ref[:, 2 * LANES : 3 * LANES] = jax.nn.sigmoid(shifted)
    weight = split3(head_lanes(jnp.exp(last - cum) * dt, heads))
    row = lax.broadcasted_iota(jnp.int32, (8, LANES), 0)
    edges = jnp.where(row == 0, jnp.exp(total[...]), jnp.exp(jnp.broadcast_to(last, (8, LANES))))
    edges = dot(split3(head_lanes(edges, heads)), e3_ref[...])
    decay_ref[...] = edges
    total[...] = total[...] + last

    for j in range(0, conv, LANES):
        xb = pre_ref[:, j : j + LANES].astype(BF16)
        xp_ref[:, j : j + LANES] = xb
        pad[8 : 8 + TB, j : j + LANES] = xb.astype(F32)
    for j in list(range(width, conv, LANES)) + list(range(0, width, LANES)):
        xa = jnp.broadcast_to(taps_ref[4:5, j : j + LANES], (TB, LANES))
        for k in range(4):
            xa = xa + taps_ref[k : k + 1, j : j + LANES] * pad[5 + k : 5 + k + TB, j : j + LANES]
        sig = jax.nn.sigmoid(xa)
        act = (xa * sig).astype(BF16)
        xbc_ref[:, j : j + LANES] = act
        slope_ref[:, j : j + LANES] = (sig * (1.0 + xa * (1.0 - sig))).astype(BF16)
        if j < width:
            entering = state[:, j : j + LANES]
            state_ref[:, j : j + LANES] = entering
            wx = (dot(weight, e3_ref[:, j : j + LANES]) * act.astype(F32)).astype(BF16)
            fresh = dot_c0(xbc_ref[:, width : width + LANES], wx)
            leaving = edges[1:2, j : j + LANES] * entering + fresh
            state[:, j : j + LANES] = leaving
            final_ref[:, j : j + LANES] = leaving


def forward_states(pre, halo, taps, head, e3, heads, width):
    rows, full = pre.shape
    conv = full - LANES
    blocks = rows // TB
    block = lambda w: pl.BlockSpec((TB, w), lambda b: (b, 0))
    whole = lambda a: pl.BlockSpec(a.shape, lambda b: (0, 0))
    return pl.pallas_call(
        functools.partial(forward_states_kernel, heads, width),
        grid=(blocks,),
        in_specs=[block(full), whole(halo), whole(taps), whole(head), whole(e3)],
        out_specs=[
            block(conv), block(conv), block(conv), block(3 * LANES), block(width),
            pl.BlockSpec((LANES, width), lambda b: (0, 0)),
            pl.BlockSpec((8, width), lambda b: (b, 0)),
        ],
        out_shape=[
            jax.ShapeDtypeStruct((rows, conv), BF16),
            jax.ShapeDtypeStruct((rows, conv), BF16),
            jax.ShapeDtypeStruct((rows, conv), BF16),
            jax.ShapeDtypeStruct((rows, 3 * LANES), F32),
            jax.ShapeDtypeStruct((blocks * LANES, width), F32),
            jax.ShapeDtypeStruct((LANES, width), F32),
            jax.ShapeDtypeStruct((8 * blocks, width), F32),
        ],
        scratch_shapes=[
            pltpu.VMEM((TB + 8, conv), F32),
            pltpu.VMEM((LANES, width), F32),
            pltpu.VMEM((8, LANES), F32),
        ],
        name="forward_states",
    )(pre, halo, taps, head, e3)


def decay_matrix(cum, cum_t, h):
    return jnp.exp(jnp.minimum(cum[:, h : h + 1] - cum_t[h : h + 1, :], 0.0))


def forward_outputs_kernel(
    heads, width, xbc_ref, dt_ref, state_ref, carry_ref, decay_ref, z_ref, dyn_ref,
    chan_ref, e3_ref, y_ref, enter_ref, sums_ref,
):
    write = xbc_ref[:, width : width + LANES]
    read = xbc_ref[:, width + LANES : width + 2 * LANES]
    dt = split3(dt_ref[:, 0:LANES])
    cum = dt_ref[:, LANES : 2 * LANES]
    grown = split3(head_lanes(jnp.exp(cum), heads))
    cum_t = cum.T
    scores = jnp.where(tri(False), dot_t(read, write), 0.0)
    low = low_lanes()
    squares = jnp.zeros((TB, LANES), F32)
    inner = jnp.zeros((TB, LANES), F32)
    for j in range(0, width, LANES):
        h = j // 64
        sl = slice(j, j + LANES)
        x = xbc_ref[:, sl].astype(F32)
        xd = (dot(dt, e3_ref[:, sl]) * x).astype(BF16)
        entering = (state_ref[:, sl] + decay_ref[0:1, sl] * carry_ref[:, sl]).astype(BF16)
        enter_ref[:, sl] = entering
        mix = jnp.concatenate(
            [(scores * decay_matrix(cum, cum_t, h + q)).astype(BF16) for q in range(2)], axis=1
        )
        y = dot(mix, cut_pair(xd, low))
        y = y + dot(grown, e3_ref[:, sl]) * dot(read, entering)
        y = y + chan_ref[0:1, sl] * x
        y_ref[:, sl] = y
        z = z_ref[:, sl]
        gated = y * (z * jax.nn.sigmoid(z))
        squares = squares + gated * gated
        inner = inner + dyn_ref[:, sl] * chan_ref[1:2, sl] * gated
    row = lax.broadcasted_iota(jnp.int32, (8, TB), 0)
    sq = jnp.sum(squares.T, axis=0, keepdims=True)
    dots = jnp.sum(inner.T, axis=0, keepdims=True)
    sums_ref[...] = jnp.where(row == 0, sq, jnp.where(row == 1, dots, 0.0))


def forward_outputs(xbc, dt, state, carry, decay, z, dyn, chan, e3, heads, width):
    rows, conv = xbc.shape
    blocks = rows // TB
    block = lambda w: pl.BlockSpec((TB, w), lambda b: (b, 0))
    whole = lambda a: pl.BlockSpec(a.shape, lambda b: (0, 0))
    return pl.pallas_call(
        functools.partial(forward_outputs_kernel, heads, width),
        grid=(blocks,),
        in_specs=[
            block(conv), block(3 * LANES), block(width), whole(carry),
            pl.BlockSpec((8, width), lambda b: (b, 0)), block(width), block(width),
            whole(chan), whole(e3),
        ],
        out_specs=[block(width), block(width), pl.BlockSpec((8, TB), lambda b: (0, b))],
        out_shape=[
            jax.ShapeDtypeStruct((rows, width), F32),
            jax.ShapeDtypeStruct((blocks * LANES, width), BF16),
            jax.ShapeDtypeStruct((8, rows), F32),
        ],
        name="forward_outputs",
    )(xbc, dt, state, carry, decay, z, dyn, chan, e3)


def backward_states_kernel(
    heads, width, total_inner, xbc_ref, dt_ref, y_ref, z_ref, dyn_ref, sums_ref, chan_ref, e3_ref,
    yn_ref, dssd_ref, dz_ref, gain_ref, dstate_ref, dfinal_ref, decay_ref,
    dstate, total,
):
    i = pl.program_id(0)

    @pl.when(i == 0)
    def _():
        dstate[...] = jnp.zeros_like(dstate)
        total[...] = jnp.zeros_like(total)
        gain_ref[...] = jnp.zeros_like(gain_ref)

    read = xbc_ref[:, width + LANES : width + 2 * LANES]
    cum = dt_ref[:, LANES : 2 * LANES]
    last = cum[TB - 1 : TB, :]
    grown = split3(head_lanes(jnp.exp(cum), heads))
    row = lax.broadcasted_iota(jnp.int32, (8, LANES), 0)
    edges = jnp.where(row == 0, jnp.exp(total[...]), jnp.exp(jnp.broadcast_to(last, (8, LANES))))
    edges = dot(split3(head_lanes(edges, heads)), e3_ref[...])
    decay_ref[...] = edges
    total[...] = total[...] + last
    scale_row = lax.rsqrt(sums_ref[0:1, :] / total_inner + EPS)
    inner_row = sums_ref[1:2, :] / total_inner
    scale = jnp.broadcast_to(scale_row, (TB, TB)).T
    inner = jnp.broadcast_to(scale_row * scale_row * scale_row * inner_row, (TB, TB)).T
    for j in range(0, width, LANES):
        sl = slice(j, j + LANES)
        y = y_ref[:, sl]
        z = z_ref[:, sl]
        dyn = dyn_ref[:, sl]
        gain = chan_ref[1:2, sl]
        sig = jax.nn.sigmoid(z)
        act = z * sig
        gated = y * act
        scaled = gated * scale
        yn_ref[:, sl] = (scaled * gain).astype(BF16)
        gain_ref[:, sl] += rows8(dyn * scaled)
        dgated = scale * (dyn * gain) - gated * inner
        dssd = (dgated * act).astype(BF16)
        dssd_ref[:, sl] = dssd
        slope = sig * (1.0 + z * (1.0 - sig))
        dz_ref[:, sl] = (dgated * y * slope).astype(BF16)
        edy = (dot(grown, e3_ref[:, sl]) * dssd.astype(F32)).astype(BF16)
        leaving = dstate[:, sl]
        dstate_ref[:, sl] = leaving
        entering = edges[1:2, sl] * leaving + dot_c0(read, edy)
        dstate[:, sl] = entering
        dfinal_ref[:, sl] = entering


def backward_states(xbc, dt, y, z, dyn, sums, chan, e3, heads, width, total_inner):
    rows, conv = xbc.shape
    blocks = rows // TB
    back = blocks - 1
    block = lambda w: pl.BlockSpec((TB, w), lambda i: (back - i, 0))
    whole = lambda a: pl.BlockSpec(a.shape, lambda i: (0, 0))
    return pl.pallas_call(
        functools.partial(backward_states_kernel, heads, width, float(total_inner)),
        grid=(blocks,),
        in_specs=[
            block(conv), block(3 * LANES), block(width), block(width), block(width),
            pl.BlockSpec((8, TB), lambda i: (0, back - i)), whole(chan), whole(e3),
        ],
        out_specs=[
            block(width), block(width), block(width),
            pl.BlockSpec((8, width), lambda i: (0, 0)),
            block(width),
            pl.BlockSpec((LANES, width), lambda i: (0, 0)),
            pl.BlockSpec((8, width), lambda i: (back - i, 0)),
        ],
        out_shape=[
            jax.ShapeDtypeStruct((rows, width), BF16),
            jax.ShapeDtypeStruct((rows, width), BF16),
            jax.ShapeDtypeStruct((rows, width), BF16),
            jax.ShapeDtypeStruct((8, width), F32),
            jax.ShapeDtypeStruct((blocks * LANES, width), F32),
            jax.ShapeDtypeStruct((LANES, width), F32),
            jax.ShapeDtypeStruct((8 * blocks, width), F32),
        ],
        scratch_shapes=[pltpu.VMEM((LANES, width), F32), pltpu.VMEM((8, LANES), F32)],
        name="backward_states",
    )(xbc, dt, y, z, dyn, sums, chan, e3)


def backward_inputs_kernel(
    heads, width, reaches_start, xbc_ref, xp_ref, slope_ref, dt_ref, y_ref, dssd_ref, enter_ref,
    dstate_ref, dcarry_ref, decay_ref, next_ref, halo_ref, taps_ref, head_ref, chan_ref, e3_ref,
    dpre_ref, tail_ref, first_ref, rim_ref, conv_ref, headg_ref, skip_ref,
    pad, rim, grown_dy, weighted_x, dleave,
):
    i = pl.program_id(0)
    conv = xp_ref.shape[1]

    @pl.when(i == 0)
    def _():
        pad[TB : TB + 8, :] = next_ref[...]
        conv_ref[...] = jnp.zeros_like(conv_ref)
        headg_ref[...] = jnp.zeros_like(headg_ref)
        skip_ref[...] = jnp.zeros_like(skip_ref)

    @pl.when(i > 0)
    def _():
        pad[TB : TB + 8, :] = pad[0:8, :]

    write = xbc_ref[:, width : width + LANES]
    read = xbc_ref[:, width + LANES : width + 2 * LANES]
    dt_own = dt_ref[:, 0:LANES]
    cum = dt_ref[:, LANES : 2 * LANES]
    last = cum[TB - 1 : TB, :]
    dt = split3(dt_own)
    grown = split3(head_lanes(jnp.exp(cum), heads))
    fading = split3(head_lanes(jnp.exp(last - cum), heads))
    cum_t = cum.T
    causal = tri(False)
    scores = jnp.where(causal, dot_t(read, write), 0.0)
    low = low_lanes()
    dscores = jnp.zeros((TB, TB), F32)
    e1 = e3_ref[0:SLOT, :]
    dcum = jnp.zeros((TB, SLOT), F32)
    ddt = jnp.zeros((TB, SLOT), F32)
    through = jnp.zeros((8, SLOT), F32)

    def head_sum(v, sl):
        high = v.astype(BF16)
        rest = (v - high.astype(F32)).astype(BF16)
        return dot_t(high, e1[:, sl]) + dot_t(rest, e1[:, sl])

    for j in range(0, width, LANES):
        h = j // 64
        sl = slice(j, j + LANES)
        xb = xbc_ref[:, sl]
        x = xb.astype(F32)
        dyb = dssd_ref[:, sl]
        dy = dyb.astype(F32)
        dt_wide = dot(dt, e3_ref[:, sl])
        fading_wide = dot(fading, e3_ref[:, sl])
        xdb = (dt_wide * x).astype(BF16)
        xd = xdb.astype(F32)
        dy_cut = cut_pair(dyb, low)
        dmix = dot_t(dy_cut, xdb)
        mixes = []
        for q in range(2):
            fade = decay_matrix(cum, cum_t, h + q)
            dscores = dscores + dmix[q * TB : (q + 1) * TB] * fade
            mixes.append((scores * fade).astype(BF16))
        dxd = dot_c0(jnp.concatenate(mixes, axis=0), dy_cut)
        leave = dstate_ref[:, sl] + decay_ref[0:1, sl] * dcarry_ref[:, sl]
        leaveb = leave.astype(BF16)
        dleave[:, sl] = leaveb
        tail = fading_wide * dot(write, leaveb)
        dxd = dxd + tail
        skip = chan_ref[0:1, sl]
        dx = dt_wide * dxd + skip * dy
        pad[0:TB, sl] = dx * slope_ref[:, sl].astype(F32)
        grown_dy[:, sl] = (dot(grown, e3_ref[:, sl]) * dy).astype(BF16)
        weighted_x[:, sl] = (fading_wide * dt_wide * x).astype(BF16)
        dcum = dcum + head_sum(dy * (y_ref[:, sl] - skip * x) - xd * dxd, sl)
        ddt = ddt + head_sum(x * dxd, sl)
        enter = enter_ref[:, sl].astype(F32)
        edge = rows8(xd * tail) + rows8(leave * enter) * decay_ref[1:2, sl]
        through = through + head_sum(edge, sl)
        skip_ref[:, sl] += rows8(dy * x)

    dscores = jnp.where(causal, dscores, 0.0).astype(BF16)
    dread = dot(dscores, write) + dot_t(grown_dy[...], enter_ref[...])
    dwrite = dot_c0(dscores, read) + dot_t(weighted_x[...], dleave[...])
    pad[0:TB, width : width + LANES] = dwrite * slope_ref[:, width : width + LANES].astype(F32)
    pad[0:TB, width + LANES : conv] = dread * slope_ref[:, width + LANES : conv].astype(F32)

    blank = jnp.zeros((TB, LANES - SLOT), F32)
    dcum = jnp.concatenate([dcum, blank], axis=1)
    ddt = jnp.concatenate([ddt, blank], axis=1)
    through = jnp.concatenate([jnp.sum(through, axis=0, keepdims=True), blank[0:1]], axis=1)
    dla = join3(dot(tri(True).astype(F32).astype(BF16), split3(dcum)))
    dla = head_lanes(dla + through, heads)
    ddt = ddt + head_ref[1:2, :] * dla
    du = head_lanes(ddt * dt_ref[:, 2 * LANES : 3 * LANES], heads)
    dpre_ref[:, conv : conv + LANES] = du.astype(BF16)
    headg_ref[0:8, :] += rows8(du)
    headg_ref[8:16, :] += rows8(dla * dt_own)

    for j in range(0, conv, LANES):
        sl = slice(j, j + LANES)
        xp = xp_ref[:, sl].astype(F32)
        dxp = jnp.zeros((TB, LANES), F32)
        for k in range(4):
            piece = pad[3 - k : 3 - k + TB, sl]
            dxp = dxp + taps_ref[k : k + 1, sl] * piece
            conv_ref[8 * k : 8 * k + 8, sl] += rows8(xp * piece)
            if k == 3:
                conv_ref[32:40, sl] += rows8(piece)
        dpre_ref[:, sl] = dxp.astype(BF16)

        @pl.when(i == 0)
        def _():
            tail_ref[:, sl] = dxp[TB - 8 : TB]

    @pl.when(i == pl.num_programs(0) - 1)
    def _():
        first_ref[...] = pad[0:8, :]
        rim[0:8, :] = jnp.zeros((8, conv), F32)
        rim[8:16, :] = pad[0:8, :]
        xp = halo_ref[:, 0:conv].astype(BF16).astype(F32)
        out = jnp.zeros((8, conv), F32)
        for k in range(4):
            piece = rim[3 - k : 11 - k, :]
            out = out + taps_ref[k : k + 1, :] * piece
            if reaches_start:
                conv_ref[8 * k : 8 * k + 8, :] += xp * piece
        rim_ref[...] = out


def backward_inputs(
    xbc, xp, slope, dt, y, dssd, enter, dstate, dcarry, decay, after, halo, taps, head, chan, e3,
    heads, width, start, blocks,
):
    conv = xbc.shape[1]
    rows = blocks * TB
    back = start + blocks - 1
    block = lambda w: pl.BlockSpec((TB, w), lambda i: (back - i, 0))
    whole = lambda a: pl.BlockSpec(a.shape, lambda i: (0, 0))
    kept = lambda r, w: pl.BlockSpec((r, w), lambda i: (0, 0))
    return pl.pallas_call(
        functools.partial(backward_inputs_kernel, heads, width, start == 0),
        grid=(blocks,),
        in_specs=[
            block(conv), block(conv), block(conv), block(3 * LANES), block(width), block(width),
            block(width), block(width), whole(dcarry),
            pl.BlockSpec((8, width), lambda i: (back - i, 0)),
            whole(after), whole(halo), whole(taps), whole(head), whole(chan), whole(e3),
        ],
        out_specs=[
            pl.BlockSpec((TB, conv + LANES), lambda i: (blocks - 1 - i, 0)),
            kept(8, conv), kept(8, conv), kept(8, conv), kept(40, conv),
            kept(16, LANES), kept(8, width),
        ],
        out_shape=[
            jax.ShapeDtypeStruct((rows, conv + LANES), BF16),
            jax.ShapeDtypeStruct((8, conv), F32),
            jax.ShapeDtypeStruct((8, conv), F32),
            jax.ShapeDtypeStruct((8, conv), F32),
            jax.ShapeDtypeStruct((40, conv), F32),
            jax.ShapeDtypeStruct((16, LANES), F32),
            jax.ShapeDtypeStruct((8, width), F32),
        ],
        scratch_shapes=[
            pltpu.VMEM((TB + 8, conv), F32),
            pltpu.VMEM((16, conv), F32),
            pltpu.VMEM((TB, width), BF16),
            pltpu.VMEM((TB, width), BF16),
            pltpu.VMEM((LANES, width), BF16),
        ],
        name="backward_inputs",
    )(
        xbc, xp, slope, dt, y, dssd, enter, dstate, dcarry, decay, after, halo, taps, head, chan,
        e3,
    )


def finish_kernel(axis, count, steps, aliased, own_ref, h_ref, cot_ref, gain_ref, *rest):
    arrived, rest = rest[: 2 * (count - 1)], rest[2 * (count - 1) + aliased :]
    out_ref, got, sems = rest
    rows, model = own_ref.shape
    place = lax.axis_index(axis)
    ranks = (place, count - 1 - place)
    now = pl.program_id(0)

    def copy(side, i, step):
        at = pl.ds(step * rows, rows)
        return pltpu.make_async_copy(
            arrived[side * (count - 1) + i - 1].at[at], got.at[side, at], sems.at[side, step]
        )

    @pl.when(now == 0)
    def _():
        for side, rank in enumerate(ranks):
            for i in range(1, count):

                @pl.when(rank == i)
                def _():
                    for step in range(steps):
                        copy(side, i, step).start()

            @pl.when(rank == 0)
            def _():
                got[side] = jnp.zeros((steps * rows, model), BF16)

    for side, rank in enumerate(ranks):
        for i in range(1, count):

            @pl.when(rank == i)
            def _():
                copy(side, i, now).wait()

    gain = gain_ref[0:1, :]
    first = now * rows
    for k in range(0, rows, 16):
        at = pl.ds(k, 16)
        there = pl.ds(pl.multiple_of(first + k, 16), 16)
        hf = h_ref[at, :].astype(F32)
        inverse = lax.rsqrt(jnp.sum(hf * hf, axis=-1, keepdims=True) / model + EPS)
        total = own_ref[at, :].astype(F32) + got[0, there, :].astype(F32)
        weighted = (total + got[1, there, :].astype(F32)) * gain
        inner = jnp.sum(weighted * hf, axis=-1, keepdims=True) / model
        out_ref[at, :] = (
            cot_ref[at, :].astype(F32) + inverse * weighted
            - hf * (inverse * inverse * inverse * inner)
        )


def finish(chunk, chunks, own, h, cot, gain, right, left, so_far):
    rows, model = own.shape[0] // chunks, own.shape[1]
    steps = 4
    piece = rows // steps
    count = len(right) + 1
    anywhere = pl.BlockSpec(memory_space=pl.ANY)
    block = pl.BlockSpec((piece, model), lambda i: (chunk * steps + i, 0))
    operands = [own, h, cot, gain, *right, *left]
    specs = [
        block, block, block,
        pl.BlockSpec(gain.shape, lambda i: (0, 0)),
    ] + [anywhere] * (2 * (count - 1))
    aliases = {}
    if so_far is not None:
        aliases = {len(operands): 0}
        operands.append(so_far)
        specs.append(anywhere)
    return pl.pallas_call(
        functools.partial(finish_kernel, "ta", count, steps, so_far is not None),
        grid=(steps,),
        in_specs=specs,
        out_specs=block,
        out_shape=jax.ShapeDtypeStruct(h.shape, F32),
        scratch_shapes=[pltpu.VMEM((2, rows, model), BF16), pltpu.SemaphoreType.DMA((2, steps))],
        input_output_aliases=aliases,
        name="finish",
    )(*operands)


def outer(left, right):
    return lax.dot_general(left, right, (((0,), (0,)), ((), ())), preferred_element_type=F32)


def against(left, right):
    return lax.dot_general(left, right, (((1,), (1,)), ((), ())), preferred_element_type=F32)


def product(left, right):
    return jnp.dot(left, right, preferred_element_type=F32)


def row_of(values, width):
    return jnp.pad(values.astype(F32), (0, width - values.shape[0]))[None, :]


def program(
    hidden, lengths, norm_gain, gate_proj, input_proj, state_proj, step_proj, conv_input,
    conv_input_bias, conv_state, conv_state_bias, step_bias, decay_log, skip_gain, gated_gain,
    output_proj, cotangent,
):
    _, positions, model = hidden.shape
    heads = step_bias.shape[0]
    width = gated_gain.shape[0]
    both = state_proj.shape[1]
    conv = width + both
    local_rows = norm_gain.shape[0]
    total_inner = width * lax.axis_size("ta")
    h = hidden[0]
    cot = cotangent[0]

    packed = jnp.concatenate(
        [
            input_proj, state_proj, step_proj,
            jnp.zeros((local_rows, LANES - heads), BF16),
        ],
        axis=1,
    )
    halo_h = shifted_by(h[positions - 8 :], "col", 1)
    (packed_full,) = gather_rows(packed, [packed.shape[1]])
    gate_full = lax.all_gather(gate_proj, ("af", "col"), axis=0, tiled=True)
    output_full = lax.all_gather(output_proj, ("af", "col"), axis=0, tiled=True)
    gain = gather_vector(norm_gain)

    e3 = (
        (jnp.arange(LANES)[:, None] % SLOT == jnp.arange(width)[None, :] // (width // heads))
        & (jnp.arange(LANES)[:, None] < 3 * SLOT)
    ).astype(BF16)
    taps = jnp.concatenate(
        [
            jnp.concatenate([conv_input, conv_state], axis=1),
            jnp.concatenate([conv_input_bias, conv_state_bias])[None, :],
            jnp.zeros((3, conv), F32),
        ],
        axis=0,
    )
    rate = -jnp.exp(decay_log)
    head = jnp.concatenate(
        [row_of(step_bias, LANES), row_of(rate, LANES), jnp.zeros((6, LANES), F32)], axis=0
    )
    chan = jnp.concatenate(
        [
            jnp.repeat(skip_gain, width // heads)[None, :], gated_gain[None, :],
            jnp.zeros((6, width), F32),
        ],
        axis=0,
    )

    def normalise(rows):
        values = rows.astype(F32)
        inverse = lax.rsqrt(jnp.mean(values * values, axis=-1, keepdims=True) + EPS)
        return lax.optimization_barrier((values * inverse * gain).astype(BF16))

    normed = normalise(h)
    halo_normed = normalise(halo_h)
    pre = product(normed, packed_full)
    halo = product(halo_normed, packed_full)
    xp, xbc, slope, dt, state, final, decay = forward_states(
        pre, halo, taps, head, e3, heads, width
    )
    carry = shifted_by(final, "col", 1)
    z = product(normed, gate_full)

    position = lax.axis_index("col") * positions + jnp.arange(positions)
    valid = (position < lengths[0]).astype(F32)[:, None]
    dmix = (cot.astype(F32) * valid).astype(BF16)
    dyn = product(dmix, output_full)
    y, enter, sums = forward_outputs(xbc, dt, state, carry, decay, z, dyn, chan, e3, heads, width)
    sums = sum_over(sums, "ta")
    yn, dssd, dz, gain_part, dstate, dfinal, fade = backward_states(
        xbc, dt, y, z, dyn, sums, chan, e3, heads, width, total_inner
    )
    dcarry = shifted_by(dfinal, "col", -1)

    mixed = against(output_full, yn).astype(BF16)
    mixed = lax.psum_scatter(mixed, "ta", scatter_dimension=0, tiled=True)
    quarter = mixed.shape[0]
    own = lax.dynamic_slice_in_dim(h, lax.axis_index("ta") * quarter, quarter, 1).astype(F32)
    block_out = (own + mixed.T.astype(F32) * valid).astype(BF16)

    dpre, tail, _, rim, conv_part, head_part, skip_part = backward_inputs(
        xbc, xp, slope, dt, y, dssd, enter, dstate, dcarry, fade, jnp.zeros((8, conv), F32),
        halo, taps, head, chan, e3, heads, width, 0, positions // TB,
    )
    tail = (tail + shifted_by(rim, "col", -1)).astype(BF16)
    dpre = lax.dynamic_update_slice(dpre, tail, (positions - 8, 0))
    partial = (against(dz, gate_full) + against(dpre, packed_full)).astype(BF16)

    chunks = 4
    count = lax.axis_size("ta")
    gain_rows = jnp.broadcast_to(gain, (8, model))
    hidden_grad, arrived = None, []
    for tick in range(chunks + count - 2):
        arrived.append(
            chain_sum_step(
                partial, "ta", tick, chunks, arrived[-1] if arrived else None,
                mixed if tick == 1 else None,
            )
        )
        at = tick - count + 2
        if at >= 0:
            came = arrived[at : at + count - 1]
            hidden_grad = finish(
                at, chunks, partial, h, cot, gain_rows, [v[0] for v in came],
                [v[1] for v in came], hidden_grad,
            )

    def scattered(value):
        return lax.psum_scatter(
            value.astype(BF16), ("af", "col"), scatter_dimension=0, tiled=True
        ).astype(F32)

    output_grad = outer(dmix, yn)
    gate_grad = outer(normed, dz)
    output_grad = scattered(output_grad)
    gate_grad = scattered(gate_grad)
    packed_grad = outer(normed, dpre).astype(BF16)
    packed_grad = scatter_rows(packed_grad)

    input_grad = packed_grad[:, :width]
    state_grad = packed_grad[:, width:conv]
    step_grad = packed_grad[:, conv : conv + heads]
    rows_dot = (
        jnp.sum(gate_grad * gate_proj.astype(F32), axis=1)
        + jnp.sum(input_grad * input_proj.astype(F32), axis=1)
        + jnp.sum(state_grad * state_proj.astype(F32), axis=1)
        + jnp.sum(step_grad * step_proj.astype(F32), axis=1)
    )

    conv_sums = jnp.sum(conv_part.reshape(5, 8, conv), axis=1)
    head_sums = jnp.sum(head_part.reshape(2, 8, LANES), axis=1)
    small = jnp.concatenate(
        [
            jnp.pad(conv_sums, ((0, 0), (0, LANES * 2))),
            jnp.concatenate(
                [
                    jnp.sum(gain_part, axis=0), jnp.zeros((both,), F32), head_sums[0], head_sums[1],
                ]
            )[None, :],
            jnp.pad(jnp.sum(skip_part, axis=0), (0, both + 2 * LANES))[None, :],
            jnp.zeros((1, conv + 2 * LANES), F32),
        ],
        axis=0,
    )
    small = sum_over(sum_over(small, "col"), "af")
    third = jnp.concatenate(
        [state_grad, jnp.broadcast_to(rows_dot[:, None], (local_rows, LANES))], axis=1
    )
    third = jnp.concatenate([third, jnp.pad(small[:, width:conv], ((0, 0), (0, LANES)))], axis=0)
    third = sum_over(third, "ta")
    state_grad = third[:local_rows, :both]
    norm_gain_grad = third[:local_rows, both] / norm_gain.astype(F32)
    state_small = third[local_rows:, :both]
    skip_grad = jnp.sum(small[6, :width].reshape(heads, width // heads), axis=1)
    return (
        block_out[None],
        hidden_grad[None],
        norm_gain_grad,
        gate_grad,
        input_grad,
        state_grad,
        step_grad,
        small[0:4, :width],
        small[4, :width],
        state_small[0:4],
        state_small[4],
        small[5, conv : conv + heads],
        rate * small[5, conv + LANES : conv + LANES + heads],
        skip_grad,
        small[5, :width],
        output_grad,
    )


def solution(mesh):
    return mapped(mesh)


def mapped(mesh):
    return jax.shard_map(
        program,
        mesh=mesh,
        in_specs=(
            P("af", "col", None),
            P("af"),
            P(("af", "col")),
            P(("af", "col"), "ta"),
            P(("af", "col"), "ta"),
            P(("af", "col"), None),
            P(("af", "col"), "ta"),
            P(None, "ta"),
            P("ta"),
            P(),
            P(),
            P("ta"),
            P("ta"),
            P("ta"),
            P("ta"),
            P(("af", "col"), "ta"),
            P("af", "col", None),
        ),
        out_specs=(
            P("af", "col", "ta"),
            P("af", "col", None),
            P(("af", "col")),
            P(("af", "col"), "ta"),
            P(("af", "col"), "ta"),
            P(("af", "col"), None),
            P(("af", "col"), "ta"),
            P(None, "ta"),
            P("ta"),
            P(),
            P(),
            P("ta"),
            P("ta"),
            P("ta"),
            P("ta"),
            P(("af", "col"), "ta"),
        ),
        check_vma=False,
    )
```

```python
import functools

import jax
import jax.numpy as jnp
from jax import lax
from jax.experimental import pallas as pl
from jax.experimental.pallas import tpu as pltpu
from jax.sharding import PartitionSpec as P


EPS = 1e-05
TB = 128
LANES = 128
SLOT = 16
GRANT = 52 * 1024 * 1024
F32 = jnp.float32
BF16 = jnp.bfloat16


def bit_pairs(axis, bit):
    count = lax.axis_size(axis)
    return [(i, i ^ (1 << bit)) for i in range(count)]


def swap_bit(value, axis, bit):
    return lax.ppermute(value, axis, bit_pairs(axis, bit))


def own_bit(axis, bit):
    return (lax.axis_index(axis) >> bit) & 1


def bits_of(axis):
    return lax.axis_size(axis).bit_length() - 1


def shifted_by(value, axis, steps):
    count = lax.axis_size(axis)
    return lax.ppermute(
        value, axis, [(i, i + steps) for i in range(count) if 0 <= i + steps < count]
    )


def pick(value, index, axis):
    return lax.dynamic_index_in_dim(value, index, axis, False)


def spread_bits(block, axis, order):
    bits = bits_of(axis)
    value = block.reshape((1,) * bits + block.shape)
    for bit in order:
        other = swap_bit(value, axis, bit)
        mine = own_bit(axis, bit)
        dim = bits - 1 - bit
        value = jnp.where(
            mine == 0,
            jnp.concatenate([value, other], axis=dim),
            jnp.concatenate([other, value], axis=dim),
        )
    return value


def place_kernel(splits, where_ref, *refs):
    pieces, outs = refs[:10], refs[10:]
    place = where_ref[1]
    half = pieces[3].shape[0]
    now = pl.program_id(0)
    for which in range(2):
        own, x, y, upper, lower = pieces[5 * which : 5 * which + 5]
        slot = place if which == 0 else 1 - place
        for relative, source in enumerate((own, x, y, None)):

            @pl.when(now == relative)
            def _():
                for (start, stop), out in zip(splits, outs):
                    if source is None:
                        out[pl.ds(slot, 1), 0:half, :] = upper[:, start:stop][None]
                        out[pl.ds(slot, 1), half:, :] = lower[:, start:stop][None]
                    else:
                        out[pl.ds(slot, 1)] = source[:, start:stop][None]


def place_rows(mine, other, widths):
    rows, _ = mine[0].shape
    edges = [sum(widths[:k]) for k in range(len(widths) + 1)]
    where = jnp.stack([lax.axis_index("af"), lax.axis_index("col")]).astype(jnp.int32)
    pieces = list(mine) + list(other)
    outs = pl.pallas_call(
        functools.partial(place_kernel, list(zip(edges[:-1], edges[1:]))),
        grid_spec=pltpu.PrefetchScalarGridSpec(
            num_scalar_prefetch=1,
            grid=(4,),
            in_specs=[pl.BlockSpec(piece.shape, lambda i, at: (0, 0)) for piece in pieces],
            out_specs=[
                pl.BlockSpec((2, rows, w), lambda i, at: (at[0] ^ i, 0, 0)) for w in widths
            ],
        ),
        out_shape=[jax.ShapeDtypeStruct((8, rows, w), mine[0].dtype) for w in widths],
        name="place_rows",
        compiler_params=pltpu.CompilerParams(vmem_limit_bytes=GRANT),
    )(where, *pieces)
    return [out.reshape(8 * rows, out.shape[2]) for out in outs]


def gather_rows(local, widths):
    rows, width = local.shape
    half = rows // 2
    if bits_of("af") == 2:
        x = swap_bit(local, "af", 0)
        y = swap_bit(local, "af", 1)
        upper = swap_bit(x[:half], "af", 1)
        lower = swap_bit(y[half:], "af", 0)
        mine = (local, x, y, upper, lower)
        other = [swap_bit(v, "col", 0) for v in mine]
        return place_rows(mine, other, widths)
    order = list(range(bits_of("af")))
    count = lax.axis_size("af")
    first = spread_bits(local[:half], "af", order).reshape(count, half, width)
    second = spread_bits(local[half:], "af", order[::-1]).reshape(count, half, width)
    mine = jnp.concatenate([first, second], axis=1)
    other = swap_bit(mine, "col", 0)
    place = lax.axis_index("col")
    both = jnp.where(place == 0, jnp.stack([mine, other], 1), jnp.stack([other, mine], 1))
    both = both.reshape(count * 2 * rows, width)
    edges = [sum(widths[:k]) for k in range(len(widths) + 1)]
    return [both[:, i:j] for i, j in zip(edges[:-1], edges[1:])]


def gather_vector(local):
    count = lax.axis_size("af") * 2
    place = lax.axis_index("af") * 2 + lax.axis_index("col")
    own = jnp.arange(count)[:, None] == place
    whole = jnp.where(own, local.astype(F32)[None, :], 0.0).reshape(1, -1)
    return sum_over(sum_over(whole, "af"), "col")


def after(value, *others):
    return lax.optimization_barrier((value,) + others)[0]


def fold_bits(value, axis, order):
    bits = bits_of(axis)
    for bit in order:
        dim = bits - 1 - bit
        mine = own_bit(axis, bit)
        sent = lax.dynamic_slice_in_dim(value, 1 - mine, 1, dim).astype(BF16)
        kept = lax.dynamic_slice_in_dim(value, mine, 1, dim)
        value = kept.astype(F32) + swap_bit(sent, axis, bit).astype(F32)
    return value.reshape(value.shape[bits:])


def scatter_rows(whole):
    count = lax.axis_size("af")
    bits = bits_of("af")
    width = whole.shape[1]
    rows = whole.shape[0] // (2 * count)
    half = rows // 2
    place = lax.axis_index("col")
    blocks = whole.reshape(count, 2, rows, width)
    got = swap_bit(pick(blocks, 1 - place, 1).astype(BF16), "col", 0)
    summed = pick(blocks, place, 1).astype(F32) + got.astype(F32)
    order = list(range(bits))
    lead = (2,) * bits
    first = fold_bits(summed[:, :half].reshape(lead + (half, width)), "af", order)
    second = fold_bits(summed[:, half:].reshape(lead + (half, width)), "af", order[::-1])
    return jnp.concatenate([first, second], axis=0)


def sum_over(value, axis):
    for bit in range(bits_of(axis)):
        value = value + swap_bit(value, axis, bit)
    return value


def chain_sum_step(part, axis, tick, chunks, got, needed=None):
    count = lax.axis_size(axis)
    place = lax.axis_index(axis)
    rows = part.shape[0] // chunks
    sends, pairs = [], []
    for side, step in enumerate((1, -1)):
        rank = place if step == 1 else count - 1 - place
        senders = [i for i in range(count - 1) if 0 <= tick - i < chunks]
        if len(senders) == 1:
            index = tick - senders[0]
        else:
            index = jnp.clip(tick - rank, 0, chunks - 1)
        sent = lax.dynamic_slice_in_dim(part, index * rows, rows, 0)
        if got is not None:
            sent = (sent.astype(F32) + got[side].astype(F32)).astype(BF16)
        sends.append(sent)
        pairs.append(
            [(i, i + 1) if step == 1 else (count - 1 - i, count - 2 - i) for i in senders]
        )
    extra = () if needed is None else (needed,)
    sends = lax.optimization_barrier(tuple(sends) + extra)[:2]
    out = [lax.ppermute(sends[side], axis, pairs[side]) for side in range(2)]
    return lax.optimization_barrier(tuple(out))


def dot(a, b):
    return jnp.dot(a, b, preferred_element_type=F32)


def dot_t(a, b):
    return lax.dot_general(a, b, (((1,), (1,)), ((), ())), preferred_element_type=F32)


def dot_c0(a, b):
    return lax.dot_general(a, b, (((0,), (0,)), ((), ())), preferred_element_type=F32)


def split3(v):
    high = v.astype(BF16).astype(F32)
    rest = v - high
    middle = rest.astype(BF16).astype(F32)
    low = rest - middle
    return (high + pltpu.roll(middle, SLOT, 1) + pltpu.roll(low, 2 * SLOT, 1)).astype(BF16)


def join3(v):
    return v + pltpu.roll(v, LANES - SLOT, 1) + pltpu.roll(v, LANES - 2 * SLOT, 1)


def head_lanes(v, heads):
    lane = lax.broadcasted_iota(jnp.int32, v.shape, 1)
    return jnp.where(lane < heads, v, 0.0)


def tri(upper):
    row = lax.broadcasted_iota(jnp.int32, (TB, TB), 0)
    col = lax.broadcasted_iota(jnp.int32, (TB, TB), 1)
    return (row <= col) if upper else (row >= col)


def rows8(v):
    out = v[0:8]
    for k in range(8, v.shape[0], 8):
        out = out + v[k : k + 8]
    return out


def low_lanes():
    return lax.broadcasted_iota(jnp.int32, (TB, LANES), 1) < 64


def cut_pair(v, low):
    zero = jnp.zeros_like(v)
    return jnp.concatenate([jnp.where(low, v, zero), jnp.where(low, zero, v)], axis=0)


def forward_states_kernel(
    heads, width, pre_ref, halo_ref, taps_ref, head_ref, e3_ref,
    xp_ref, xbc_ref, slope_ref, dt_ref, state_ref, final_ref, decay_ref,
    pad, state, total,
):
    b = pl.program_id(0)
    conv = xp_ref.shape[1]

    @pl.when(b == 0)
    def _():
        pad[0:8, :] = halo_ref[:, 0:conv].astype(BF16).astype(F32)
        state[...] = jnp.zeros_like(state)
        total[...] = jnp.zeros_like(total)

    @pl.when(b > 0)
    def _():
        pad[0:8, :] = pad[TB : TB + 8, :]

    shifted = pre_ref[:, conv : conv + LANES] + head_ref[0:1, :]
    dt = head_lanes(jax.nn.softplus(shifted), heads)
    la = dt * head_ref[1:2, :]
    cum = head_lanes(join3(dot(tri(False).astype(F32).astype(BF16), split3(la))), heads)
    last = cum[TB - 1 : TB, :]
    dt_ref[:, 0:LANES] = dt
    dt_ref[:, LANES : 2 * LANES] = cum
    dt_ref[:, 2 * LANES : 3 * LANES] = jax.nn.sigmoid(shifted)
    weight = split3(head_lanes(jnp.exp(last - cum) * dt, heads))
    row = lax.broadcasted_iota(jnp.int32, (8, LANES), 0)
    edges = jnp.where(row == 0, jnp.exp(total[...]), jnp.exp(jnp.broadcast_to(last, (8, LANES))))
    edges = dot(split3(head_lanes(edges, heads)), e3_ref[...])
    decay_ref[...] = edges
    total[...] = total[...] + last

    for j in range(0, conv, LANES):
        xb = pre_ref[:, j : j + LANES].astype(BF16)
        xp_ref[:, j : j + LANES] = xb
        pad[8 : 8 + TB, j : j + LANES] = xb.astype(F32)
    for j in list(range(width, conv, LANES)) + list(range(0, width, LANES)):
        xa = jnp.broadcast_to(taps_ref[4:5, j : j + LANES], (TB, LANES))
        for k in range(4):
            xa = xa + taps_ref[k : k + 1, j : j + LANES] * pad[5 + k : 5 + k + TB, j : j + LANES]
        sig = jax.nn.sigmoid(xa)
        act = (xa * sig).astype(BF16)
        xbc_ref[:, j : j + LANES] = act
        slope_ref[:, j : j + LANES] = (sig * (1.0 + xa * (1.0 - sig))).astype(BF16)
        if j < width:
            entering = state[:, j : j + LANES]
            state_ref[:, j : j + LANES] = entering
            wx = (dot(weight, e3_ref[:, j : j + LANES]) * act.astype(F32)).astype(BF16)
            fresh = dot_c0(xbc_ref[:, width : width + LANES], wx)
            leaving = edges[1:2, j : j + LANES] * entering + fresh
            state[:, j : j + LANES] = leaving
            final_ref[:, j : j + LANES] = leaving


def forward_states(pre, halo, taps, head, e3, heads, width):
    rows, full = pre.shape
    conv = full - LANES
    blocks = rows // TB
    block = lambda w: pl.BlockSpec((TB, w), lambda b: (b, 0))
    whole = lambda a: pl.BlockSpec(a.shape, lambda b: (0, 0))
    return pl.pallas_call(
        functools.partial(forward_states_kernel, heads, width),
        grid=(blocks,),
        in_specs=[block(full), whole(halo), whole(taps), whole(head), whole(e3)],
        out_specs=[
            block(conv), block(conv), block(conv), block(3 * LANES), block(width),
            pl.BlockSpec((LANES, width), lambda b: (0, 0)),
            pl.BlockSpec((8, width), lambda b: (b, 0)),
        ],
        out_shape=[
            jax.ShapeDtypeStruct((rows, conv), BF16),
            jax.ShapeDtypeStruct((rows, conv), BF16),
            jax.ShapeDtypeStruct((rows, conv), BF16),
            jax.ShapeDtypeStruct((rows, 3 * LANES), F32),
            jax.ShapeDtypeStruct((blocks * LANES, width), F32),
            jax.ShapeDtypeStruct((LANES, width), F32),
            jax.ShapeDtypeStruct((8 * blocks, width), F32),
        ],
        scratch_shapes=[
            pltpu.VMEM((TB + 8, conv), F32),
            pltpu.VMEM((LANES, width), F32),
            pltpu.VMEM((8, LANES), F32),
        ],
        name="forward_states",
        compiler_params=pltpu.CompilerParams(vmem_limit_bytes=GRANT),
    )(pre, halo, taps, head, e3)


def decay_matrix(cum, cum_t, h):
    return jnp.exp(jnp.minimum(cum[:, h : h + 1] - cum_t[h : h + 1, :], 0.0))


def forward_outputs_kernel(
    heads, width, xbc_ref, dt_ref, state_ref, carry_ref, decay_ref, z_ref, dyn_ref,
    chan_ref, e3_ref, y_ref, enter_ref, sums_ref,
):
    write = xbc_ref[:, width : width + LANES]
    read = xbc_ref[:, width + LANES : width + 2 * LANES]
    dt = split3(dt_ref[:, 0:LANES])
    cum = dt_ref[:, LANES : 2 * LANES]
    grown = split3(head_lanes(jnp.exp(cum), heads))
    cum_t = cum.T
    scores = jnp.where(tri(False), dot_t(read, write), 0.0)
    low = low_lanes()
    squares = jnp.zeros((TB, LANES), F32)
    inner = jnp.zeros((TB, LANES), F32)
    for j in range(0, width, LANES):
        h = j // 64
        sl = slice(j, j + LANES)
        x = xbc_ref[:, sl].astype(F32)
        xd = (dot(dt, e3_ref[:, sl]) * x).astype(BF16)
        entering = (state_ref[:, sl] + decay_ref[0:1, sl] * carry_ref[:, sl]).astype(BF16)
        enter_ref[:, sl] = entering
        mix = jnp.concatenate(
            [(scores * decay_matrix(cum, cum_t, h + q)).astype(BF16) for q in range(2)], axis=1
        )
        y = dot(mix, cut_pair(xd, low))
        y = y + dot(grown, e3_ref[:, sl]) * dot(read, entering)
        y = y + chan_ref[0:1, sl] * x
        y_ref[:, sl] = y
        z = z_ref[:, sl]
        gated = y * (z * jax.nn.sigmoid(z))
        squares = squares + gated * gated
        inner = inner + dyn_ref[:, sl] * chan_ref[1:2, sl] * gated
    row = lax.broadcasted_iota(jnp.int32, (8, TB), 0)
    sq = jnp.sum(squares.T, axis=0, keepdims=True)
    dots = jnp.sum(inner.T, axis=0, keepdims=True)
    sums_ref[...] = jnp.where(row == 0, sq, jnp.where(row == 1, dots, 0.0))


def forward_outputs(xbc, dt, state, carry, decay, z, dyn, chan, e3, heads, width):
    rows, conv = xbc.shape
    blocks = rows // TB
    block = lambda w: pl.BlockSpec((TB, w), lambda b: (b, 0))
    whole = lambda a: pl.BlockSpec(a.shape, lambda b: (0, 0))
    return pl.pallas_call(
        functools.partial(forward_outputs_kernel, heads, width),
        grid=(blocks,),
        in_specs=[
            block(conv), block(3 * LANES), block(width), whole(carry),
            pl.BlockSpec((8, width), lambda b: (b, 0)), block(width), block(width),
            whole(chan), whole(e3),
        ],
        out_specs=[block(width), block(width), pl.BlockSpec((8, TB), lambda b: (0, b))],
        out_shape=[
            jax.ShapeDtypeStruct((rows, width), F32),
            jax.ShapeDtypeStruct((blocks * LANES, width), BF16),
            jax.ShapeDtypeStruct((8, rows), F32),
        ],
        name="forward_outputs",
        compiler_params=pltpu.CompilerParams(vmem_limit_bytes=GRANT),
    )(xbc, dt, state, carry, decay, z, dyn, chan, e3)


def backward_states_kernel(
    heads, width, total_inner, xbc_ref, dt_ref, y_ref, z_ref, dyn_ref, sums_ref, chan_ref, e3_ref,
    yn_ref, dssd_ref, dz_ref, gain_ref, dstate_ref, dfinal_ref, decay_ref,
    dstate, total,
):
    i = pl.program_id(0)

    @pl.when(i == 0)
    def _():
        dstate[...] = jnp.zeros_like(dstate)
        total[...] = jnp.zeros_like(total)
        gain_ref[...] = jnp.zeros_like(gain_ref)

    read = xbc_ref[:, width + LANES : width + 2 * LANES]
    cum = dt_ref[:, LANES : 2 * LANES]
    last = cum[TB - 1 : TB, :]
    grown = split3(head_lanes(jnp.exp(cum), heads))
    row = lax.broadcasted_iota(jnp.int32, (8, LANES), 0)
    edges = jnp.where(row == 0, jnp.exp(total[...]), jnp.exp(jnp.broadcast_to(last, (8, LANES))))
    edges = dot(split3(head_lanes(edges, heads)), e3_ref[...])
    decay_ref[...] = edges
    total[...] = total[...] + last
    scale_row = lax.rsqrt(sums_ref[0:1, :] / total_inner + EPS)
    inner_row = sums_ref[1:2, :] / total_inner
    scale = jnp.broadcast_to(scale_row, (TB, TB)).T
    inner = jnp.broadcast_to(scale_row * scale_row * scale_row * inner_row, (TB, TB)).T
    for j in range(0, width, LANES):
        sl = slice(j, j + LANES)
        y = y_ref[:, sl]
        z = z_ref[:, sl]
        dyn = dyn_ref[:, sl]
        gain = chan_ref[1:2, sl]
        sig = jax.nn.sigmoid(z)
        act = z * sig
        gated = y * act
        scaled = gated * scale
        yn_ref[:, sl] = (scaled * gain).astype(BF16)
        gain_ref[:, sl] += rows8(dyn * scaled)
        dgated = scale * (dyn * gain) - gated * inner
        dssd = (dgated * act).astype(BF16)
        dssd_ref[:, sl] = dssd
        slope = sig * (1.0 + z * (1.0 - sig))
        dz_ref[:, sl] = (dgated * y * slope).astype(BF16)
        edy = (dot(grown, e3_ref[:, sl]) * dssd.astype(F32)).astype(BF16)
        leaving = dstate[:, sl]
        dstate_ref[:, sl] = leaving
        entering = edges[1:2, sl] * leaving + dot_c0(read, edy)
        dstate[:, sl] = entering
        dfinal_ref[:, sl] = entering


def backward_states(xbc, dt, y, z, dyn, sums, chan, e3, heads, width, total_inner):
    rows, conv = xbc.shape
    blocks = rows // TB
    back = blocks - 1
    block = lambda w: pl.BlockSpec((TB, w), lambda i: (back - i, 0))
    whole = lambda a: pl.BlockSpec(a.shape, lambda i: (0, 0))
    return pl.pallas_call(
        functools.partial(backward_states_kernel, heads, width, float(total_inner)),
        grid=(blocks,),
        in_specs=[
            block(conv), block(3 * LANES), block(width), block(width), block(width),
            pl.BlockSpec((8, TB), lambda i: (0, back - i)), whole(chan), whole(e3),
        ],
        out_specs=[
            block(width), block(width), block(width),
            pl.BlockSpec((8, width), lambda i: (0, 0)),
            block(width),
            pl.BlockSpec((LANES, width), lambda i: (0, 0)),
            pl.BlockSpec((8, width), lambda i: (back - i, 0)),
        ],
        out_shape=[
            jax.ShapeDtypeStruct((rows, width), BF16),
            jax.ShapeDtypeStruct((rows, width), BF16),
            jax.ShapeDtypeStruct((rows, width), BF16),
            jax.ShapeDtypeStruct((8, width), F32),
            jax.ShapeDtypeStruct((blocks * LANES, width), F32),
            jax.ShapeDtypeStruct((LANES, width), F32),
            jax.ShapeDtypeStruct((8 * blocks, width), F32),
        ],
        scratch_shapes=[pltpu.VMEM((LANES, width), F32), pltpu.VMEM((8, LANES), F32)],
        name="backward_states",
        compiler_params=pltpu.CompilerParams(vmem_limit_bytes=GRANT),
    )(xbc, dt, y, z, dyn, sums, chan, e3)


def backward_inputs_kernel(
    heads, width, reaches_start, xbc_ref, xp_ref, slope_ref, dt_ref, y_ref, dssd_ref, enter_ref,
    dstate_ref, dcarry_ref, decay_ref, next_ref, halo_ref, taps_ref, head_ref, chan_ref, e3_ref,
    dpre_ref, tail_ref, first_ref, rim_ref, conv_ref, headg_ref, skip_ref,
    pad, rim, grown_dy, weighted_x, dleave,
):
    i = pl.program_id(0)
    conv = xp_ref.shape[1]

    @pl.when(i == 0)
    def _():
        pad[TB : TB + 8, :] = next_ref[...]
        conv_ref[...] = jnp.zeros_like(conv_ref)
        headg_ref[...] = jnp.zeros_like(headg_ref)
        skip_ref[...] = jnp.zeros_like(skip_ref)

    @pl.when(i > 0)
    def _():
        pad[TB : TB + 8, :] = pad[0:8, :]

    write = xbc_ref[:, width : width + LANES]
    read = xbc_ref[:, width + LANES : width + 2 * LANES]
    dt_own = dt_ref[:, 0:LANES]
    cum = dt_ref[:, LANES : 2 * LANES]
    last = cum[TB - 1 : TB, :]
    dt = split3(dt_own)
    grown = split3(head_lanes(jnp.exp(cum), heads))
    fading = split3(head_lanes(jnp.exp(last - cum), heads))
    cum_t = cum.T
    causal = tri(False)
    scores = jnp.where(causal, dot_t(read, write), 0.0)
    low = low_lanes()
    dscores = jnp.zeros((TB, TB), F32)
    e1 = e3_ref[0:SLOT, :]
    dcum = jnp.zeros((TB, SLOT), F32)
    ddt = jnp.zeros((TB, SLOT), F32)
    through = jnp.zeros((8, SLOT), F32)

    def head_sum(v, sl):
        high = v.astype(BF16)
        rest = (v - high.astype(F32)).astype(BF16)
        return dot_t(high, e1[:, sl]) + dot_t(rest, e1[:, sl])

    for j in range(0, width, LANES):
        h = j // 64
        sl = slice(j, j + LANES)
        xb = xbc_ref[:, sl]
        x = xb.astype(F32)
        dyb = dssd_ref[:, sl]
        dy = dyb.astype(F32)
        dt_wide = dot(dt, e3_ref[:, sl])
        fading_wide = dot(fading, e3_ref[:, sl])
        xdb = (dt_wide * x).astype(BF16)
        xd = xdb.astype(F32)
        dy_cut = cut_pair(dyb, low)
        dmix = dot_t(dy_cut, xdb)
        mixes = []
        for q in range(2):
            fade = decay_matrix(cum, cum_t, h + q)
            dscores = dscores + dmix[q * TB : (q + 1) * TB] * fade
            mixes.append((scores * fade).astype(BF16))
        dxd = dot_c0(jnp.concatenate(mixes, axis=0), dy_cut)
        leave = dstate_ref[:, sl] + decay_ref[0:1, sl] * dcarry_ref[:, sl]
        leaveb = leave.astype(BF16)
        dleave[:, sl] = leaveb
        tail = fading_wide * dot(write, leaveb)
        dxd = dxd + tail
        skip = chan_ref[0:1, sl]
        dx = dt_wide * dxd + skip * dy
        pad[0:TB, sl] = dx * slope_ref[:, sl].astype(F32)
        grown_dy[:, sl] = (dot(grown, e3_ref[:, sl]) * dy).astype(BF16)
        weighted_x[:, sl] = (fading_wide * dt_wide * x).astype(BF16)
        dcum = dcum + head_sum(dy * (y_ref[:, sl] - skip * x) - xd * dxd, sl)
        ddt = ddt + head_sum(x * dxd, sl)
        enter = enter_ref[:, sl].astype(F32)
        edge = rows8(xd * tail) + rows8(leave * enter) * decay_ref[1:2, sl]
        through = through + head_sum(edge, sl)
        skip_ref[:, sl] += rows8(dy * x)

    dscores = jnp.where(causal, dscores, 0.0).astype(BF16)
    dread = dot(dscores, write) + dot_t(grown_dy[...], enter_ref[...])
    dwrite = dot_c0(dscores, read) + dot_t(weighted_x[...], dleave[...])
    pad[0:TB, width : width + LANES] = dwrite * slope_ref[:, width : width + LANES].astype(F32)
    pad[0:TB, width + LANES : conv] = dread * slope_ref[:, width + LANES : conv].astype(F32)

    blank = jnp.zeros((TB, LANES - SLOT), F32)
    dcum = jnp.concatenate([dcum, blank], axis=1)
    ddt = jnp.concatenate([ddt, blank], axis=1)
    through = jnp.concatenate([jnp.sum(through, axis=0, keepdims=True), blank[0:1]], axis=1)
    dla = join3(dot(tri(True).astype(F32).astype(BF16), split3(dcum)))
    dla = head_lanes(dla + through, heads)
    ddt = ddt + head_ref[1:2, :] * dla
    du = head_lanes(ddt * dt_ref[:, 2 * LANES : 3 * LANES], heads)
    dpre_ref[:, conv : conv + LANES] = du.astype(BF16)
    headg_ref[0:8, :] += rows8(du)
    headg_ref[8:16, :] += rows8(dla * dt_own)

    for j in range(0, conv, LANES):
        sl = slice(j, j + LANES)
        xp = xp_ref[:, sl].astype(F32)
        dxp = jnp.zeros((TB, LANES), F32)
        for k in range(4):
            piece = pad[3 - k : 3 - k + TB, sl]
            dxp = dxp + taps_ref[k : k + 1, sl] * piece
            conv_ref[8 * k : 8 * k + 8, sl] += rows8(xp * piece)
            if k == 3:
                conv_ref[32:40, sl] += rows8(piece)
        dpre_ref[:, sl] = dxp.astype(BF16)

        @pl.when(i == 0)
        def _():
            tail_ref[:, sl] = dxp[TB - 8 : TB]

    @pl.when(i == pl.num_programs(0) - 1)
    def _():
        first_ref[...] = pad[0:8, :]
        rim[0:8, :] = jnp.zeros((8, conv), F32)
        rim[8:16, :] = pad[0:8, :]
        xp = halo_ref[:, 0:conv].astype(BF16).astype(F32)
        out = jnp.zeros((8, conv), F32)
        for k in range(4):
            piece = rim[3 - k : 11 - k, :]
            out = out + taps_ref[k : k + 1, :] * piece
            if reaches_start:
                conv_ref[8 * k : 8 * k + 8, :] += xp * piece
        rim_ref[...] = out


def backward_inputs(
    xbc, xp, slope, dt, y, dssd, enter, dstate, dcarry, decay, after, halo, taps, head, chan, e3,
    heads, width, start, blocks,
):
    conv = xbc.shape[1]
    rows = blocks * TB
    back = start + blocks - 1
    block = lambda w: pl.BlockSpec((TB, w), lambda i: (back - i, 0))
    whole = lambda a: pl.BlockSpec(a.shape, lambda i: (0, 0))
    kept = lambda r, w: pl.BlockSpec((r, w), lambda i: (0, 0))
    return pl.pallas_call(
        functools.partial(backward_inputs_kernel, heads, width, start == 0),
        grid=(blocks,),
        in_specs=[
            block(conv), block(conv), block(conv), block(3 * LANES), block(width), block(width),
            block(width), block(width), whole(dcarry),
            pl.BlockSpec((8, width), lambda i: (back - i, 0)),
            whole(after), whole(halo), whole(taps), whole(head), whole(chan), whole(e3),
        ],
        out_specs=[
            pl.BlockSpec((TB, conv + LANES), lambda i: (blocks - 1 - i, 0)),
            kept(8, conv), kept(8, conv), kept(8, conv), kept(40, conv),
            kept(16, LANES), kept(8, width),
        ],
        out_shape=[
            jax.ShapeDtypeStruct((rows, conv + LANES), BF16),
            jax.ShapeDtypeStruct((8, conv), F32),
            jax.ShapeDtypeStruct((8, conv), F32),
            jax.ShapeDtypeStruct((8, conv), F32),
            jax.ShapeDtypeStruct((40, conv), F32),
            jax.ShapeDtypeStruct((16, LANES), F32),
            jax.ShapeDtypeStruct((8, width), F32),
        ],
        scratch_shapes=[
            pltpu.VMEM((TB + 8, conv), F32),
            pltpu.VMEM((16, conv), F32),
            pltpu.VMEM((TB, width), BF16),
            pltpu.VMEM((TB, width), BF16),
            pltpu.VMEM((LANES, width), BF16),
        ],
        name="backward_inputs",
        compiler_params=pltpu.CompilerParams(vmem_limit_bytes=GRANT),
    )(
        xbc, xp, slope, dt, y, dssd, enter, dstate, dcarry, decay, after, halo, taps, head, chan,
        e3,
    )


def finish_kernel(axis, count, steps, aliased, own_ref, h_ref, cot_ref, gain_ref, *rest):
    arrived, rest = rest[: 2 * (count - 1)], rest[2 * (count - 1) + aliased :]
    out_ref, got, sems = rest
    rows, model = own_ref.shape
    place = lax.axis_index(axis)
    ranks = (place, count - 1 - place)
    now = pl.program_id(0)

    def copy(side, i, step):
        at = pl.ds(step * rows, rows)
        return pltpu.make_async_copy(
            arrived[side * (count - 1) + i - 1].at[at], got.at[side, at], sems.at[side, step]
        )

    @pl.when(now == 0)
    def _():
        for side, rank in enumerate(ranks):
            for i in range(1, count):

                @pl.when(rank == i)
                def _():
                    for step in range(steps):
                        copy(side, i, step).start()

            @pl.when(rank == 0)
            def _():
                got[side] = jnp.zeros((steps * rows, model), BF16)

    for side, rank in enumerate(ranks):
        for i in range(1, count):

            @pl.when(rank == i)
            def _():
                copy(side, i, now).wait()

    gain = gain_ref[0:1, :]
    first = now * rows
    for k in range(0, rows, 16):
        at = pl.ds(k, 16)
        there = pl.ds(pl.multiple_of(first + k, 16), 16)
        hf = h_ref[at, :].astype(F32)
        inverse = lax.rsqrt(jnp.sum(hf * hf, axis=-1, keepdims=True) / model + EPS)
        total = own_ref[at, :].astype(F32) + got[0, there, :].astype(F32)
        weighted = (total + got[1, there, :].astype(F32)) * gain
        inner = jnp.sum(weighted * hf, axis=-1, keepdims=True) / model
        out_ref[at, :] = (
            cot_ref[at, :].astype(F32) + inverse * weighted
            - hf * (inverse * inverse * inverse * inner)
        )


def finish(chunk, chunks, own, h, cot, gain, right, left, so_far):
    rows, model = own.shape[0] // chunks, own.shape[1]
    steps = 2
    piece = rows // steps
    count = len(right) + 1
    anywhere = pl.BlockSpec(memory_space=pl.ANY)
    block = pl.BlockSpec((piece, model), lambda i: (chunk * steps + i, 0))
    operands = [own, h, cot, gain, *right, *left]
    specs = [
        block, block, block,
        pl.BlockSpec(gain.shape, lambda i: (0, 0)),
    ] + [anywhere] * (2 * (count - 1))
    aliases = {}
    if so_far is not None:
        aliases = {len(operands): 0}
        operands.append(so_far)
        specs.append(anywhere)
    return pl.pallas_call(
        functools.partial(finish_kernel, "ta", count, steps, so_far is not None),
        grid=(steps,),
        in_specs=specs,
        out_specs=block,
        out_shape=jax.ShapeDtypeStruct(h.shape, F32),
        scratch_shapes=[pltpu.VMEM((2, rows, model), BF16), pltpu.SemaphoreType.DMA((2, steps))],
        input_output_aliases=aliases,
        name="finish",
        compiler_params=pltpu.CompilerParams(vmem_limit_bytes=GRANT),
    )(*operands)


def outer(left, right):
    return lax.dot_general(left, right, (((0,), (0,)), ((), ())), preferred_element_type=F32)


def against(left, right):
    return lax.dot_general(left, right, (((1,), (1,)), ((), ())), preferred_element_type=F32)


def product(left, right):
    return jnp.dot(left, right, preferred_element_type=F32)


def row_of(values, width):
    return jnp.pad(values.astype(F32), (0, width - values.shape[0]))[None, :]


def program(
    hidden, lengths, norm_gain, gate_proj, input_proj, state_proj, step_proj, conv_input,
    conv_input_bias, conv_state, conv_state_bias, step_bias, decay_log, skip_gain, gated_gain,
    output_proj, cotangent,
):
    _, positions, model = hidden.shape
    heads = step_bias.shape[0]
    width = gated_gain.shape[0]
    both = state_proj.shape[1]
    conv = width + both
    local_rows = norm_gain.shape[0]
    total_inner = width * lax.axis_size("ta")
    h = hidden[0]
    cot = cotangent[0]

    packed = jnp.concatenate(
        [
            input_proj, state_proj, step_proj,
            jnp.zeros((local_rows, LANES - heads), BF16),
        ],
        axis=1,
    )
    halo_h = shifted_by(h[positions - 8 :], "col", 1)
    (packed_full,) = gather_rows(packed, [packed.shape[1]])
    gate_full = lax.all_gather(gate_proj, ("af", "col"), axis=0, tiled=True)
    output_full = lax.all_gather(output_proj, ("af", "col"), axis=0, tiled=True)
    gain = gather_vector(norm_gain)

    e3 = (
        (jnp.arange(LANES)[:, None] % SLOT == jnp.arange(width)[None, :] // (width // heads))
        & (jnp.arange(LANES)[:, None] < 3 * SLOT)
    ).astype(BF16)
    taps = jnp.concatenate(
        [
            jnp.concatenate([conv_input, conv_state], axis=1),
            jnp.concatenate([conv_input_bias, conv_state_bias])[None, :],
            jnp.zeros((3, conv), F32),
        ],
        axis=0,
    )
    rate = -jnp.exp(decay_log)
    head = jnp.concatenate(
        [row_of(step_bias, LANES), row_of(rate, LANES), jnp.zeros((6, LANES), F32)], axis=0
    )
    chan = jnp.concatenate(
        [
            jnp.repeat(skip_gain, width // heads)[None, :], gated_gain[None, :],
            jnp.zeros((6, width), F32),
        ],
        axis=0,
    )

    def normalise(rows):
        values = rows.astype(F32)
        inverse = lax.rsqrt(jnp.mean(values * values, axis=-1, keepdims=True) + EPS)
        return lax.optimization_barrier((values * inverse * gain).astype(BF16))

    normed = normalise(h)
    halo_normed = normalise(halo_h)
    pre = product(normed, packed_full)
    halo = product(halo_normed, packed_full)
    xp, xbc, slope, dt, state, final, decay = forward_states(
        pre, halo, taps, head, e3, heads, width
    )
    carry = shifted_by(final, "col", 1)
    z = product(normed, gate_full)

    position = lax.axis_index("col") * positions + jnp.arange(positions)
    valid = (position < lengths[0]).astype(F32)[:, None]
    dmix = (cot.astype(F32) * valid).astype(BF16)
    dyn = product(dmix, output_full)
    y, enter, sums = forward_outputs(xbc, dt, state, carry, decay, z, dyn, chan, e3, heads, width)
    sums = sum_over(sums, "ta")
    yn, dssd, dz, gain_part, dstate, dfinal, fade = backward_states(
        xbc, dt, y, z, dyn, sums, chan, e3, heads, width, total_inner
    )
    dcarry = shifted_by(dfinal, "col", -1)

    mixed = against(output_full, yn).astype(BF16)
    mixed = lax.psum_scatter(mixed, "ta", scatter_dimension=0, tiled=True)
    quarter = mixed.shape[0]
    own = lax.dynamic_slice_in_dim(h, lax.axis_index("ta") * quarter, quarter, 1).astype(F32)
    block_out = (own + mixed.T.astype(F32) * valid).astype(BF16)

    dpre, tail, _, rim, conv_part, head_part, skip_part = backward_inputs(
        xbc, xp, slope, dt, y, dssd, enter, dstate, dcarry, fade, jnp.zeros((8, conv), F32),
        halo, taps, head, chan, e3, heads, width, 0, positions // TB,
    )
    tail = (tail + shifted_by(rim, "col", -1)).astype(BF16)
    dpre = lax.dynamic_update_slice(dpre, tail, (positions - 8, 0))
    partial = (against(dz, gate_full) + against(dpre, packed_full)).astype(BF16)

    chunks = 4
    count = lax.axis_size("ta")
    gain_rows = jnp.broadcast_to(gain, (8, model))
    hidden_grad, arrived = None, []
    for tick in range(chunks + count - 2):
        arrived.append(
            chain_sum_step(
                partial, "ta", tick, chunks, arrived[-1] if arrived else None,
                mixed if tick == 1 else None,
            )
        )
        at = tick - count + 2
        if at >= 0:
            came = arrived[at : at + count - 1]
            hidden_grad = finish(
                at, chunks, partial, h, cot, gain_rows, [v[0] for v in came],
                [v[1] for v in came], hidden_grad,
            )

    def scattered(value):
        return lax.psum_scatter(
            value.astype(BF16), ("af", "col"), scatter_dimension=0, tiled=True
        ).astype(F32)

    output_grad = outer(dmix, yn)
    gate_grad = outer(normed, dz)
    gate_grad = scattered(after(gate_grad.astype(BF16), mixed))
    output_grad = scattered(after(output_grad.astype(BF16), gate_grad))
    packed_grad = outer(normed, dpre).astype(BF16)
    packed_grad = scatter_rows(packed_grad)

    input_grad = packed_grad[:, :width]
    state_grad = packed_grad[:, width:conv]
    step_grad = packed_grad[:, conv : conv + heads]
    rows_dot = (
        jnp.sum(gate_grad * gate_proj.astype(F32), axis=1)
        + jnp.sum(input_grad * input_proj.astype(F32), axis=1)
        + jnp.sum(state_grad * state_proj.astype(F32), axis=1)
        + jnp.sum(step_grad * step_proj.astype(F32), axis=1)
    )

    conv_sums = jnp.sum(conv_part.reshape(5, 8, conv), axis=1)
    head_sums = jnp.sum(head_part.reshape(2, 8, LANES), axis=1)
    small = jnp.concatenate(
        [
            jnp.pad(conv_sums, ((0, 0), (0, LANES * 2))),
            jnp.concatenate(
                [
                    jnp.sum(gain_part, axis=0), jnp.zeros((both,), F32), head_sums[0], head_sums[1],
                ]
            )[None, :],
            jnp.pad(jnp.sum(skip_part, axis=0), (0, both + 2 * LANES))[None, :],
            jnp.zeros((1, conv + 2 * LANES), F32),
        ],
        axis=0,
    )
    small = sum_over(sum_over(small, "col"), "af")
    gains = jnp.pad(rows_dot, (0, -local_rows % both)).reshape(-1, both)
    third = jnp.concatenate(
        [
            state_grad, small[:, width:conv], gains,
            jnp.zeros((-gains.shape[0] % 8, both), F32),
        ],
        axis=0,
    )
    third = sum_over(third, "ta")
    state_grad = third[:local_rows]
    state_small = third[local_rows:]
    gains = third[local_rows + 8 : local_rows + 8 + gains.shape[0]].reshape(-1)
    norm_gain_grad = gains[:local_rows] / norm_gain.astype(F32)
    skip_grad = jnp.sum(small[6, :width].reshape(heads, width // heads), axis=1)
    return (
        block_out[None],
        hidden_grad[None],
        norm_gain_grad,
        gate_grad,
        input_grad,
        state_grad,
        step_grad,
        small[0:4, :width],
        small[4, :width],
        state_small[0:4],
        state_small[4],
        small[5, conv : conv + heads],
        rate * small[5, conv + LANES : conv + LANES + heads],
        skip_grad,
        small[5, :width],
        output_grad,
    )


def solution(mesh):
    return mapped(mesh)


def mapped(mesh):
    return jax.shard_map(
        program,
        mesh=mesh,
        in_specs=(
            P("af", "col", None),
            P("af"),
            P(("af", "col")),
            P(("af", "col"), "ta"),
            P(("af", "col"), "ta"),
            P(("af", "col"), None),
            P(("af", "col"), "ta"),
            P(None, "ta"),
            P("ta"),
            P(),
            P(),
            P("ta"),
            P("ta"),
            P("ta"),
            P("ta"),
            P(("af", "col"), "ta"),
            P("af", "col", None),
        ),
        out_specs=(
            P("af", "col", "ta"),
            P("af", "col", None),
            P(("af", "col")),
            P(("af", "col"), "ta"),
            P(("af", "col"), "ta"),
            P(("af", "col"), None),
            P(("af", "col"), "ta"),
            P(None, "ta"),
            P("ta"),
            P(),
            P(),
            P("ta"),
            P("ta"),
            P("ta"),
            P("ta"),
            P(("af", "col"), "ta"),
        ),
        check_vma=False,
    )
```

```python
import functools

import jax
import jax.numpy as jnp
from jax import lax
from jax.experimental import pallas as pl
from jax.experimental.layout import Layout, with_layout_constraint
from jax.experimental.pallas import tpu as pltpu
from jax.sharding import PartitionSpec as P


EPS = 1e-05
TB = 128
LANES = 128
SLOT = 16
GRANT = 52 * 1024 * 1024
F32 = jnp.float32
BF16 = jnp.bfloat16


def bit_pairs(axis, bit):
    count = lax.axis_size(axis)
    return [(i, i ^ (1 << bit)) for i in range(count)]


def swap_bit(value, axis, bit):
    return lax.ppermute(value, axis, bit_pairs(axis, bit))


def own_bit(axis, bit):
    return (lax.axis_index(axis) >> bit) & 1


def bits_of(axis):
    return lax.axis_size(axis).bit_length() - 1


def shifted_by(value, axis, steps):
    count = lax.axis_size(axis)
    return lax.ppermute(
        value, axis, [(i, i + steps) for i in range(count) if 0 <= i + steps < count]
    )


def pick(value, index, axis):
    return lax.dynamic_index_in_dim(value, index, axis, False)


def spread_bits(block, axis, order):
    bits = bits_of(axis)
    value = block.reshape((1,) * bits + block.shape)
    for bit in order:
        other = swap_bit(value, axis, bit)
        mine = own_bit(axis, bit)
        dim = bits - 1 - bit
        value = jnp.where(
            mine == 0,
            jnp.concatenate([value, other], axis=dim),
            jnp.concatenate([other, value], axis=dim),
        )
    return value


def place_kernel(splits, where_ref, *refs):
    pieces, outs = refs[:10], refs[10:]
    place = where_ref[1]
    half = pieces[3].shape[0]
    now = pl.program_id(0)
    for which in range(2):
        own, x, y, upper, lower = pieces[5 * which : 5 * which + 5]
        slot = place if which == 0 else 1 - place
        for relative, source in enumerate((own, x, y, None)):

            @pl.when(now == relative)
            def _():
                for (start, stop), out in zip(splits, outs):
                    if source is None:
                        out[pl.ds(slot, 1), 0:half, :] = upper[:, start:stop][None]
                        out[pl.ds(slot, 1), half:, :] = lower[:, start:stop][None]
                    else:
                        out[pl.ds(slot, 1)] = source[:, start:stop][None]


def place_rows(mine, other, widths):
    rows, _ = mine[0].shape
    edges = [sum(widths[:k]) for k in range(len(widths) + 1)]
    where = jnp.stack([lax.axis_index("af"), lax.axis_index("col")]).astype(jnp.int32)
    pieces = list(mine) + list(other)
    outs = pl.pallas_call(
        functools.partial(place_kernel, list(zip(edges[:-1], edges[1:]))),
        grid_spec=pltpu.PrefetchScalarGridSpec(
            num_scalar_prefetch=1,
            grid=(4,),
            in_specs=[pl.BlockSpec(piece.shape, lambda i, at: (0, 0)) for piece in pieces],
            out_specs=[
                pl.BlockSpec((2, rows, w), lambda i, at: (at[0] ^ i, 0, 0)) for w in widths
            ],
        ),
        out_shape=[jax.ShapeDtypeStruct((8, rows, w), mine[0].dtype) for w in widths],
        name="place_rows",
        compiler_params=pltpu.CompilerParams(vmem_limit_bytes=GRANT),
    )(where, *pieces)
    return [out.reshape(8 * rows, out.shape[2]) for out in outs]


def gather_rows(local, widths):
    rows, width = local.shape
    half = rows // 2
    if bits_of("af") == 2:
        x = swap_bit(local, "af", 0)
        y = swap_bit(local, "af", 1)
        upper = swap_bit(x[:half], "af", 1)
        lower = swap_bit(y[half:], "af", 0)
        mine = (local, x, y, upper, lower)
        other = [swap_bit(v, "col", 0) for v in mine]
        return place_rows(mine, other, widths)
    order = list(range(bits_of("af")))
    count = lax.axis_size("af")
    first = spread_bits(local[:half], "af", order).reshape(count, half, width)
    second = spread_bits(local[half:], "af", order[::-1]).reshape(count, half, width)
    mine = jnp.concatenate([first, second], axis=1)
    other = swap_bit(mine, "col", 0)
    place = lax.axis_index("col")
    both = jnp.where(place == 0, jnp.stack([mine, other], 1), jnp.stack([other, mine], 1))
    both = both.reshape(count * 2 * rows, width)
    edges = [sum(widths[:k]) for k in range(len(widths) + 1)]
    return [both[:, i:j] for i, j in zip(edges[:-1], edges[1:])]


def gather_vector(local):
    count = lax.axis_size("af") * 2
    place = lax.axis_index("af") * 2 + lax.axis_index("col")
    own = jnp.arange(count)[:, None] == place
    whole = jnp.where(own, local.astype(F32)[None, :], 0.0).reshape(1, -1)
    return sum_over(sum_over(whole, "af"), "col")


def after(value, *others):
    return lax.optimization_barrier((value,) + others)[0]


def fold_bits(value, axis, order):
    bits = bits_of(axis)
    for bit in order:
        dim = bits - 1 - bit
        mine = own_bit(axis, bit)
        sent = lax.dynamic_slice_in_dim(value, 1 - mine, 1, dim).astype(BF16)
        kept = lax.dynamic_slice_in_dim(value, mine, 1, dim)
        value = kept.astype(F32) + swap_bit(sent, axis, bit).astype(F32)
    return value.reshape(value.shape[bits:])


def scatter_rows(whole):
    count = lax.axis_size("af")
    bits = bits_of("af")
    width = whole.shape[1]
    rows = whole.shape[0] // (2 * count)
    half = rows // 2
    place = lax.axis_index("col")
    blocks = whole.reshape(count, 2, rows, width)
    got = swap_bit(pick(blocks, 1 - place, 1).astype(BF16), "col", 0)
    summed = pick(blocks, place, 1).astype(F32) + got.astype(F32)
    order = list(range(bits))
    lead = (2,) * bits
    first = fold_bits(summed[:, :half].reshape(lead + (half, width)), "af", order)
    second = fold_bits(summed[:, half:].reshape(lead + (half, width)), "af", order[::-1])
    return jnp.concatenate([first, second], axis=0)


def sum_over(value, axis):
    for bit in range(bits_of(axis)):
        value = value + swap_bit(value, axis, bit)
    return value


def chain_sum_step(part, axis, tick, chunks, got, needed=None):
    count = lax.axis_size(axis)
    place = lax.axis_index(axis)
    rows = part.shape[0] // chunks
    sends, pairs = [], []
    for side, step in enumerate((1, -1)):
        rank = place if step == 1 else count - 1 - place
        senders = [i for i in range(count - 1) if 0 <= tick - i < chunks]
        if len(senders) == 1:
            index = tick - senders[0]
        else:
            index = jnp.clip(tick - rank, 0, chunks - 1)
        sent = lax.dynamic_slice_in_dim(part, index * rows, rows, 0)
        if got is not None:
            sent = (sent.astype(F32) + got[side].astype(F32)).astype(BF16)
        sends.append(sent)
        pairs.append(
            [(i, i + 1) if step == 1 else (count - 1 - i, count - 2 - i) for i in senders]
        )
    extra = () if needed is None else (needed,)
    sends = lax.optimization_barrier(tuple(sends) + extra)[:2]
    out = [lax.ppermute(sends[side], axis, pairs[side]) for side in range(2)]
    return lax.optimization_barrier(tuple(out))


def dot(a, b):
    return jnp.dot(a, b, preferred_element_type=F32)


def dot_t(a, b):
    return lax.dot_general(a, b, (((1,), (1,)), ((), ())), preferred_element_type=F32)


def dot_c0(a, b):
    return lax.dot_general(a, b, (((0,), (0,)), ((), ())), preferred_element_type=F32)


def split3(v):
    high = v.astype(BF16).astype(F32)
    rest = v - high
    middle = rest.astype(BF16).astype(F32)
    low = rest - middle
    return (high + pltpu.roll(middle, SLOT, 1) + pltpu.roll(low, 2 * SLOT, 1)).astype(BF16)


def join3(v):
    return v + pltpu.roll(v, LANES - SLOT, 1) + pltpu.roll(v, LANES - 2 * SLOT, 1)


def head_lanes(v, heads):
    lane = lax.broadcasted_iota(jnp.int32, v.shape, 1)
    return jnp.where(lane < heads, v, 0.0)


def tri(upper):
    row = lax.broadcasted_iota(jnp.int32, (TB, TB), 0)
    col = lax.broadcasted_iota(jnp.int32, (TB, TB), 1)
    return (row <= col) if upper else (row >= col)


def rows8(v):
    out = v[0:8]
    for k in range(8, v.shape[0], 8):
        out = out + v[k : k + 8]
    return out


def low_lanes():
    return lax.broadcasted_iota(jnp.int32, (TB, LANES), 1) < 64


def cut_pair(v, low):
    zero = jnp.zeros_like(v)
    return jnp.concatenate([jnp.where(low, v, zero), jnp.where(low, zero, v)], axis=0)


def forward_states_kernel(
    heads, width, pre_ref, halo_ref, taps_ref, head_ref, e3_ref,
    xp_ref, xbc_ref, slope_ref, dt_ref, state_ref, final_ref, decay_ref,
    pad, state, total,
):
    b = pl.program_id(0)
    conv = xp_ref.shape[1]

    @pl.when(b == 0)
    def _():
        pad[0:8, :] = halo_ref[:, 0:conv].astype(BF16).astype(F32)
        state[...] = jnp.zeros_like(state)
        total[...] = jnp.zeros_like(total)

    @pl.when(b > 0)
    def _():
        pad[0:8, :] = pad[TB : TB + 8, :]

    shifted = pre_ref[:, conv : conv + LANES] + head_ref[0:1, :]
    dt = head_lanes(jax.nn.softplus(shifted), heads)
    la = dt * head_ref[1:2, :]
    cum = head_lanes(join3(dot(tri(False).astype(F32).astype(BF16), split3(la))), heads)
    last = cum[TB - 1 : TB, :]
    dt_ref[:, 0:LANES] = dt
    dt_ref[:, LANES : 2 * LANES] = cum
    dt_ref[:, 2 * LANES : 3 * LANES] = jax.nn.sigmoid(shifted)
    weight = split3(head_lanes(jnp.exp(last - cum) * dt, heads))
    row = lax.broadcasted_iota(jnp.int32, (8, LANES), 0)
    edges = jnp.where(row == 0, jnp.exp(total[...]), jnp.exp(jnp.broadcast_to(last, (8, LANES))))
    edges = dot(split3(head_lanes(edges, heads)), e3_ref[...])
    decay_ref[...] = edges
    total[...] = total[...] + last

    for j in range(0, conv, LANES):
        xb = pre_ref[:, j : j + LANES].astype(BF16)
        xp_ref[:, j : j + LANES] = xb
        pad[8 : 8 + TB, j : j + LANES] = xb.astype(F32)
    for j in list(range(width, conv, LANES)) + list(range(0, width, LANES)):
        xa = jnp.broadcast_to(taps_ref[4:5, j : j + LANES], (TB, LANES))
        for k in range(4):
            xa = xa + taps_ref[k : k + 1, j : j + LANES] * pad[5 + k : 5 + k + TB, j : j + LANES]
        sig = jax.nn.sigmoid(xa)
        act = (xa * sig).astype(BF16)
        xbc_ref[:, j : j + LANES] = act
        slope_ref[:, j : j + LANES] = (sig * (1.0 + xa * (1.0 - sig))).astype(BF16)
        if j < width:
            entering = state[:, j : j + LANES]
            state_ref[:, j : j + LANES] = entering
            wx = (dot(weight, e3_ref[:, j : j + LANES]) * act.astype(F32)).astype(BF16)
            fresh = dot_c0(xbc_ref[:, width : width + LANES], wx)
            leaving = edges[1:2, j : j + LANES] * entering + fresh
            state[:, j : j + LANES] = leaving
            final_ref[:, j : j + LANES] = leaving


def forward_states(pre, halo, taps, head, e3, heads, width):
    rows, full = pre.shape
    conv = full - LANES
    blocks = rows // TB
    block = lambda w: pl.BlockSpec((TB, w), lambda b: (b, 0))
    whole = lambda a: pl.BlockSpec(a.shape, lambda b: (0, 0))
    return pl.pallas_call(
        functools.partial(forward_states_kernel, heads, width),
        grid=(blocks,),
        in_specs=[block(full), whole(halo), whole(taps), whole(head), whole(e3)],
        out_specs=[
            block(conv), block(conv), block(conv), block(3 * LANES), block(width),
            pl.BlockSpec((LANES, width), lambda b: (0, 0)),
            pl.BlockSpec((8, width), lambda b: (b, 0)),
        ],
        out_shape=[
            jax.ShapeDtypeStruct((rows, conv), BF16),
            jax.ShapeDtypeStruct((rows, conv), BF16),
            jax.ShapeDtypeStruct((rows, conv), BF16),
            jax.ShapeDtypeStruct((rows, 3 * LANES), F32),
            jax.ShapeDtypeStruct((blocks * LANES, width), F32),
            jax.ShapeDtypeStruct((LANES, width), F32),
            jax.ShapeDtypeStruct((8 * blocks, width), F32),
        ],
        scratch_shapes=[
            pltpu.VMEM((TB + 8, conv), F32),
            pltpu.VMEM((LANES, width), F32),
            pltpu.VMEM((8, LANES), F32),
        ],
        name="forward_states",
        compiler_params=pltpu.CompilerParams(vmem_limit_bytes=GRANT),
    )(pre, halo, taps, head, e3)


def decay_matrix(cum, cum_t, h):
    return jnp.exp(jnp.minimum(cum[:, h : h + 1] - cum_t[h : h + 1, :], 0.0))


def forward_outputs_kernel(
    heads, width, xbc_ref, dt_ref, state_ref, carry_ref, decay_ref, z_ref, dyn_ref,
    chan_ref, e3_ref, y_ref, enter_ref, sums_ref,
):
    write = xbc_ref[:, width : width + LANES]
    read = xbc_ref[:, width + LANES : width + 2 * LANES]
    dt = split3(dt_ref[:, 0:LANES])
    cum = dt_ref[:, LANES : 2 * LANES]
    grown = split3(head_lanes(jnp.exp(cum), heads))
    cum_t = cum.T
    scores = jnp.where(tri(False), dot_t(read, write), 0.0)
    low = low_lanes()
    squares = jnp.zeros((TB, LANES), F32)
    inner = jnp.zeros((TB, LANES), F32)
    for j in range(0, width, LANES):
        h = j // 64
        sl = slice(j, j + LANES)
        x = xbc_ref[:, sl].astype(F32)
        xd = (dot(dt, e3_ref[:, sl]) * x).astype(BF16)
        entering = (state_ref[:, sl] + decay_ref[0:1, sl] * carry_ref[:, sl]).astype(BF16)
        enter_ref[:, sl] = entering
        mix = jnp.concatenate(
            [(scores * decay_matrix(cum, cum_t, h + q)).astype(BF16) for q in range(2)], axis=1
        )
        y = dot(mix, cut_pair(xd, low))
        y = y + dot(grown, e3_ref[:, sl]) * dot(read, entering)
        y = y + chan_ref[0:1, sl] * x
        y_ref[:, sl] = y
        z = z_ref[:, sl]
        gated = y * (z * jax.nn.sigmoid(z))
        squares = squares + gated * gated
        inner = inner + dyn_ref[:, sl] * chan_ref[1:2, sl] * gated
    row = lax.broadcasted_iota(jnp.int32, (8, TB), 0)
    sq = jnp.sum(squares.T, axis=0, keepdims=True)
    dots = jnp.sum(inner.T, axis=0, keepdims=True)
    sums_ref[...] = jnp.where(row == 0, sq, jnp.where(row == 1, dots, 0.0))


def forward_outputs(xbc, dt, state, carry, decay, z, dyn, chan, e3, heads, width):
    rows, conv = xbc.shape
    blocks = rows // TB
    block = lambda w: pl.BlockSpec((TB, w), lambda b: (b, 0))
    whole = lambda a: pl.BlockSpec(a.shape, lambda b: (0, 0))
    return pl.pallas_call(
        functools.partial(forward_outputs_kernel, heads, width),
        grid=(blocks,),
        in_specs=[
            block(conv), block(2 * LANES), block(width), whole(carry),
            pl.BlockSpec((8, width), lambda b: (b, 0)), block(width), block(width),
            whole(chan), whole(e3),
        ],
        out_specs=[block(width), block(width), pl.BlockSpec((8, TB), lambda b: (0, b))],
        out_shape=[
            jax.ShapeDtypeStruct((rows, width), F32),
            jax.ShapeDtypeStruct((blocks * LANES, width), BF16),
            jax.ShapeDtypeStruct((8, rows), F32),
        ],
        name="forward_outputs",
        compiler_params=pltpu.CompilerParams(vmem_limit_bytes=GRANT),
    )(xbc, dt, state, carry, decay, z, dyn, chan, e3)


def backward_states_kernel(
    heads, width, total_inner, read_ref, cum_ref, y_ref, z_ref, dyn_ref, sums_ref, chan_ref, e3_ref,
    yn_ref, dssd_ref, dz_ref, gain_ref, dstate_ref, dfinal_ref, decay_ref,
    dstate, total,
):
    i = pl.program_id(0)

    @pl.when(i == 0)
    def _():
        dstate[...] = jnp.zeros_like(dstate)
        total[...] = jnp.zeros_like(total)
        gain_ref[...] = jnp.zeros_like(gain_ref)

    read = read_ref[...]
    cum = cum_ref[...]
    last = cum[TB - 1 : TB, :]
    grown = split3(head_lanes(jnp.exp(cum), heads))
    row = lax.broadcasted_iota(jnp.int32, (8, LANES), 0)
    edges = jnp.where(row == 0, jnp.exp(total[...]), jnp.exp(jnp.broadcast_to(last, (8, LANES))))
    edges = dot(split3(head_lanes(edges, heads)), e3_ref[...])
    decay_ref[...] = edges
    total[...] = total[...] + last
    scale_row = lax.rsqrt(sums_ref[0:1, :] / total_inner + EPS)
    inner_row = sums_ref[1:2, :] / total_inner
    scale = jnp.broadcast_to(scale_row, (TB, TB)).T
    inner = jnp.broadcast_to(scale_row * scale_row * scale_row * inner_row, (TB, TB)).T
    for j in range(0, width, LANES):
        sl = slice(j, j + LANES)
        y = y_ref[:, sl]
        z = z_ref[:, sl]
        dyn = dyn_ref[:, sl]
        gain = chan_ref[1:2, sl]
        sig = jax.nn.sigmoid(z)
        act = z * sig
        gated = y * act
        scaled = gated * scale
        yn_ref[:, sl] = (scaled * gain).astype(BF16)
        gain_ref[:, sl] += rows8(dyn * scaled)
        dgated = scale * (dyn * gain) - gated * inner
        dssd = (dgated * act).astype(BF16)
        dssd_ref[:, sl] = dssd
        slope = sig * (1.0 + z * (1.0 - sig))
        dz_ref[:, sl] = (dgated * y * slope).astype(BF16)
        edy = (dot(grown, e3_ref[:, sl]) * dssd.astype(F32)).astype(BF16)
        leaving = dstate[:, sl]
        dstate_ref[:, sl] = leaving
        entering = edges[1:2, sl] * leaving + dot_c0(read, edy)
        dstate[:, sl] = entering
        dfinal_ref[:, sl] = entering


def backward_states(xbc, dt, y, z, dyn, sums, chan, e3, heads, width, total_inner):
    rows, _ = xbc.shape
    blocks = rows // TB
    back = blocks - 1
    block = lambda w: pl.BlockSpec((TB, w), lambda i: (back - i, 0))
    whole = lambda a: pl.BlockSpec(a.shape, lambda i: (0, 0))
    return pl.pallas_call(
        functools.partial(backward_states_kernel, heads, width, float(total_inner)),
        grid=(blocks,),
        in_specs=[
            pl.BlockSpec((TB, LANES), lambda i: (back - i, width // LANES + 1)),
            pl.BlockSpec((TB, LANES), lambda i: (back - i, 1)),
            block(width), block(width), block(width),
            pl.BlockSpec((8, TB), lambda i: (0, back - i)), whole(chan), whole(e3),
        ],
        out_specs=[
            block(width), block(width), block(width),
            pl.BlockSpec((8, width), lambda i: (0, 0)),
            block(width),
            pl.BlockSpec((LANES, width), lambda i: (0, 0)),
            pl.BlockSpec((8, width), lambda i: (back - i, 0)),
        ],
        out_shape=[
            jax.ShapeDtypeStruct((rows, width), BF16),
            jax.ShapeDtypeStruct((rows, width), BF16),
            jax.ShapeDtypeStruct((rows, width), BF16),
            jax.ShapeDtypeStruct((8, width), F32),
            jax.ShapeDtypeStruct((blocks * LANES, width), F32),
            jax.ShapeDtypeStruct((LANES, width), F32),
            jax.ShapeDtypeStruct((8 * blocks, width), F32),
        ],
        scratch_shapes=[pltpu.VMEM((LANES, width), F32), pltpu.VMEM((8, LANES), F32)],
        name="backward_states",
        compiler_params=pltpu.CompilerParams(vmem_limit_bytes=GRANT),
    )(xbc, dt, y, z, dyn, sums, chan, e3)


def backward_inputs_kernel(
    heads, width, reaches_start, xbc_ref, xp_ref, slope_ref, dt_ref, y_ref, dssd_ref, enter_ref,
    dstate_ref, dcarry_ref, decay_ref, next_ref, halo_ref, taps_ref, head_ref, chan_ref, e3_ref,
    dpre_ref, tail_ref, first_ref, rim_ref, conv_ref, headg_ref, skip_ref,
    pad, rim, grown_dy, weighted_x, dleave,
):
    i = pl.program_id(0)
    conv = xp_ref.shape[1]

    @pl.when(i == 0)
    def _():
        pad[TB : TB + 8, :] = next_ref[...]
        conv_ref[...] = jnp.zeros_like(conv_ref)
        headg_ref[...] = jnp.zeros_like(headg_ref)
        skip_ref[...] = jnp.zeros_like(skip_ref)

    @pl.when(i > 0)
    def _():
        pad[TB : TB + 8, :] = pad[0:8, :]

    write = xbc_ref[:, width : width + LANES]
    read = xbc_ref[:, width + LANES : width + 2 * LANES]
    dt_own = dt_ref[:, 0:LANES]
    cum = dt_ref[:, LANES : 2 * LANES]
    last = cum[TB - 1 : TB, :]
    dt = split3(dt_own)
    grown = split3(head_lanes(jnp.exp(cum), heads))
    fading = split3(head_lanes(jnp.exp(last - cum), heads))
    cum_t = cum.T
    causal = tri(False)
    scores = jnp.where(causal, dot_t(read, write), 0.0)
    low = low_lanes()
    dscores = jnp.zeros((TB, TB), F32)
    e1 = e3_ref[0:SLOT, :]
    dcum = jnp.zeros((TB, SLOT), F32)
    ddt = jnp.zeros((TB, SLOT), F32)
    through = jnp.zeros((8, SLOT), F32)

    def head_sum(v, sl):
        high = v.astype(BF16)
        rest = (v - high.astype(F32)).astype(BF16)
        return dot_t(high, e1[:, sl]) + dot_t(rest, e1[:, sl])

    for j in range(0, width, LANES):
        h = j // 64
        sl = slice(j, j + LANES)
        xb = xbc_ref[:, sl]
        x = xb.astype(F32)
        dyb = dssd_ref[:, sl]
        dy = dyb.astype(F32)
        dt_wide = dot(dt, e3_ref[:, sl])
        fading_wide = dot(fading, e3_ref[:, sl])
        xdb = (dt_wide * x).astype(BF16)
        xd = xdb.astype(F32)
        dy_cut = cut_pair(dyb, low)
        dmix = dot_t(dy_cut, xdb)
        mixes = []
        for q in range(2):
            fade = decay_matrix(cum, cum_t, h + q)
            dscores = dscores + dmix[q * TB : (q + 1) * TB] * fade
            mixes.append((scores * fade).astype(BF16))
        dxd = dot_c0(jnp.concatenate(mixes, axis=0), dy_cut)
        leave = dstate_ref[:, sl] + decay_ref[0:1, sl] * dcarry_ref[:, sl]
        leaveb = leave.astype(BF16)
        dleave[:, sl] = leaveb
        tail = fading_wide * dot(write, leaveb)
        dxd = dxd + tail
        skip = chan_ref[0:1, sl]
        dx = dt_wide * dxd + skip * dy
        pad[0:TB, sl] = dx * slope_ref[:, sl].astype(F32)
        grown_dy[:, sl] = (dot(grown, e3_ref[:, sl]) * dy).astype(BF16)
        weighted_x[:, sl] = (fading_wide * dt_wide * x).astype(BF16)
        dcum = dcum + head_sum(dy * (y_ref[:, sl] - skip * x) - xd * dxd, sl)
        ddt = ddt + head_sum(x * dxd, sl)
        enter = enter_ref[:, sl].astype(F32)
        edge = rows8(xd * tail) + rows8(leave * enter) * decay_ref[1:2, sl]
        through = through + head_sum(edge, sl)
        skip_ref[:, sl] += rows8(dy * x)

    dscores = jnp.where(causal, dscores, 0.0).astype(BF16)
    dread = dot(dscores, write) + dot_t(grown_dy[...], enter_ref[...])
    dwrite = dot_c0(dscores, read) + dot_t(weighted_x[...], dleave[...])
    pad[0:TB, width : width + LANES] = dwrite * slope_ref[:, width : width + LANES].astype(F32)
    pad[0:TB, width + LANES : conv] = dread * slope_ref[:, width + LANES : conv].astype(F32)

    blank = jnp.zeros((TB, LANES - SLOT), F32)
    dcum = jnp.concatenate([dcum, blank], axis=1)
    ddt = jnp.concatenate([ddt, blank], axis=1)
    through = jnp.concatenate([jnp.sum(through, axis=0, keepdims=True), blank[0:1]], axis=1)
    dla = join3(dot(tri(True).astype(F32).astype(BF16), split3(dcum)))
    dla = head_lanes(dla + through, heads)
    ddt = ddt + head_ref[1:2, :] * dla
    du = head_lanes(ddt * dt_ref[:, 2 * LANES : 3 * LANES], heads)
    dpre_ref[:, conv : conv + LANES] = du.astype(BF16)
    headg_ref[0:8, :] += rows8(du)
    headg_ref[8:16, :] += rows8(dla * dt_own)

    for j in range(0, conv, LANES):
        sl = slice(j, j + LANES)
        xp = xp_ref[:, sl].astype(F32)
        dxp = jnp.zeros((TB, LANES), F32)
        for k in range(4):
            piece = pad[3 - k : 3 - k + TB, sl]
            dxp = dxp + taps_ref[k : k + 1, sl] * piece
            conv_ref[8 * k : 8 * k + 8, sl] += rows8(xp * piece)
            if k == 3:
                conv_ref[32:40, sl] += rows8(piece)
        dpre_ref[:, sl] = dxp.astype(BF16)

        @pl.when(i == 0)
        def _():
            tail_ref[:, sl] = dxp[TB - 8 : TB]

    @pl.when(i == pl.num_programs(0) - 1)
    def _():
        first_ref[...] = pad[0:8, :]
        rim[0:8, :] = jnp.zeros((8, conv), F32)
        rim[8:16, :] = pad[0:8, :]
        xp = halo_ref[:, 0:conv].astype(BF16).astype(F32)
        out = jnp.zeros((8, conv), F32)
        for k in range(4):
            piece = rim[3 - k : 11 - k, :]
            out = out + taps_ref[k : k + 1, :] * piece
            if reaches_start:
                conv_ref[8 * k : 8 * k + 8, :] += xp * piece
        rim_ref[...] = out


def backward_inputs(
    xbc, xp, slope, dt, y, dssd, enter, dstate, dcarry, decay, after, halo, taps, head, chan, e3,
    heads, width, start, blocks,
):
    conv = xbc.shape[1]
    rows = blocks * TB
    back = start + blocks - 1
    block = lambda w: pl.BlockSpec((TB, w), lambda i: (back - i, 0))
    whole = lambda a: pl.BlockSpec(a.shape, lambda i: (0, 0))
    kept = lambda r, w: pl.BlockSpec((r, w), lambda i: (0, 0))
    return pl.pallas_call(
        functools.partial(backward_inputs_kernel, heads, width, start == 0),
        grid=(blocks,),
        in_specs=[
            block(conv), block(conv), block(conv), block(3 * LANES), block(width), block(width),
            block(width), block(width), whole(dcarry),
            pl.BlockSpec((8, width), lambda i: (back - i, 0)),
            whole(after), whole(halo), whole(taps), whole(head), whole(chan), whole(e3),
        ],
        out_specs=[
            pl.BlockSpec((TB, conv + LANES), lambda i: (blocks - 1 - i, 0)),
            kept(8, conv), kept(8, conv), kept(8, conv), kept(40, conv),
            kept(16, LANES), kept(8, width),
        ],
        out_shape=[
            jax.ShapeDtypeStruct((rows, conv + LANES), BF16),
            jax.ShapeDtypeStruct((8, conv), F32),
            jax.ShapeDtypeStruct((8, conv), F32),
            jax.ShapeDtypeStruct((8, conv), F32),
            jax.ShapeDtypeStruct((40, conv), F32),
            jax.ShapeDtypeStruct((16, LANES), F32),
            jax.ShapeDtypeStruct((8, width), F32),
        ],
        scratch_shapes=[
            pltpu.VMEM((TB + 8, conv), F32),
            pltpu.VMEM((16, conv), F32),
            pltpu.VMEM((TB, width), BF16),
            pltpu.VMEM((TB, width), BF16),
            pltpu.VMEM((LANES, width), BF16),
        ],
        name="backward_inputs",
        compiler_params=pltpu.CompilerParams(vmem_limit_bytes=GRANT),
    )(
        xbc, xp, slope, dt, y, dssd, enter, dstate, dcarry, decay, after, halo, taps, head, chan,
        e3,
    )


def finish_kernel(axis, count, steps, aliased, own_ref, h_ref, cot_ref, gain_ref, *rest):
    arrived, rest = rest[: 2 * (count - 1)], rest[2 * (count - 1) + aliased :]
    out_ref, got, sems = rest
    rows, model = own_ref.shape
    place = lax.axis_index(axis)
    ranks = (place, count - 1 - place)
    now = pl.program_id(0)

    def copy(side, i, step):
        at = pl.ds(step * rows, rows)
        return pltpu.make_async_copy(
            arrived[side * (count - 1) + i - 1].at[at], got.at[side, at], sems.at[side, step]
        )

    @pl.when(now == 0)
    def _():
        for side, rank in enumerate(ranks):
            for i in range(1, count):

                @pl.when(rank == i)
                def _():
                    for step in range(steps):
                        copy(side, i, step).start()

            @pl.when(rank == 0)
            def _():
                got[side] = jnp.zeros((steps * rows, model), BF16)

    for side, rank in enumerate(ranks):
        for i in range(1, count):

            @pl.when(rank == i)
            def _():
                copy(side, i, now).wait()

    gain = gain_ref[0:1, :]
    first = now * rows
    for k in range(0, rows, 16):
        at = pl.ds(k, 16)
        there = pl.ds(pl.multiple_of(first + k, 16), 16)
        hf = h_ref[at, :].astype(F32)
        inverse = lax.rsqrt(jnp.sum(hf * hf, axis=-1, keepdims=True) / model + EPS)
        total = own_ref[at, :].astype(F32) + got[0, there, :].astype(F32)
        weighted = (total + got[1, there, :].astype(F32)) * gain
        inner = jnp.sum(weighted * hf, axis=-1, keepdims=True) / model
        out_ref[at, :] = (
            cot_ref[at, :].astype(F32) + inverse * weighted
            - hf * (inverse * inverse * inverse * inner)
        )


def finish(chunk, chunks, own, h, cot, gain, right, left, so_far):
    rows, model = own.shape[0] // chunks, own.shape[1]
    steps = 2
    piece = rows // steps
    count = len(right) + 1
    anywhere = pl.BlockSpec(memory_space=pl.ANY)
    block = pl.BlockSpec((piece, model), lambda i: (chunk * steps + i, 0))
    operands = [own, h, cot, gain, *right, *left]
    specs = [
        block, block, block,
        pl.BlockSpec(gain.shape, lambda i: (0, 0)),
    ] + [anywhere] * (2 * (count - 1))
    aliases = {}
    if so_far is not None:
        aliases = {len(operands): 0}
        operands.append(so_far)
        specs.append(anywhere)
    return pl.pallas_call(
        functools.partial(finish_kernel, "ta", count, steps, so_far is not None),
        grid=(steps,),
        in_specs=specs,
        out_specs=block,
        out_shape=jax.ShapeDtypeStruct(h.shape, F32),
        scratch_shapes=[pltpu.VMEM((2, rows, model), BF16), pltpu.SemaphoreType.DMA((2, steps))],
        input_output_aliases=aliases,
        name="finish",
        compiler_params=pltpu.CompilerParams(vmem_limit_bytes=GRANT),
    )(*operands)


def outer(left, right):
    return lax.dot_general(left, right, (((0,), (0,)), ((), ())), preferred_element_type=F32)


def against(left, right):
    return lax.dot_general(left, right, (((1,), (1,)), ((), ())), preferred_element_type=F32)


def product(left, right):
    return jnp.dot(left, right, preferred_element_type=F32)


def row_of(values, width):
    return jnp.pad(values.astype(F32), (0, width - values.shape[0]))[None, :]


def program(
    hidden, lengths, norm_gain, gate_proj, input_proj, state_proj, step_proj, conv_input,
    conv_input_bias, conv_state, conv_state_bias, step_bias, decay_log, skip_gain, gated_gain,
    output_proj, cotangent,
):
    _, positions, model = hidden.shape
    heads = step_bias.shape[0]
    width = gated_gain.shape[0]
    both = state_proj.shape[1]
    conv = width + both
    local_rows = norm_gain.shape[0]
    total_inner = width * lax.axis_size("ta")
    h = hidden[0]
    cot = cotangent[0]

    packed = jnp.concatenate(
        [
            input_proj, state_proj, step_proj,
            jnp.zeros((local_rows, LANES - heads), BF16),
        ],
        axis=1,
    )
    halo_h = shifted_by(h[positions - 8 :], "col", 1)
    (packed_full,) = gather_rows(packed, [packed.shape[1]])
    gate_full = lax.all_gather(gate_proj, ("af", "col"), axis=0, tiled=True)
    output_full = lax.all_gather(output_proj, ("af", "col"), axis=0, tiled=True)
    gain = gather_vector(norm_gain)

    e3 = (
        (jnp.arange(LANES)[:, None] % SLOT == jnp.arange(width)[None, :] // (width // heads))
        & (jnp.arange(LANES)[:, None] < 3 * SLOT)
    ).astype(BF16)
    taps = jnp.concatenate(
        [
            jnp.concatenate([conv_input, conv_state], axis=1),
            jnp.concatenate([conv_input_bias, conv_state_bias])[None, :],
            jnp.zeros((3, conv), F32),
        ],
        axis=0,
    )
    rate = -jnp.exp(decay_log)
    head = jnp.concatenate(
        [row_of(step_bias, LANES), row_of(rate, LANES), jnp.zeros((6, LANES), F32)], axis=0
    )
    chan = jnp.concatenate(
        [
            jnp.repeat(skip_gain, width // heads)[None, :], gated_gain[None, :],
            jnp.zeros((6, width), F32),
        ],
        axis=0,
    )

    def normalise(rows):
        values = rows.astype(F32)
        inverse = lax.rsqrt(jnp.mean(values * values, axis=-1, keepdims=True) + EPS)
        return lax.optimization_barrier((values * inverse * gain).astype(BF16))

    normed = normalise(h)
    halo_normed = normalise(halo_h)
    pre = product(normed, packed_full)
    halo = product(halo_normed, packed_full)
    xp, xbc, slope, dt, state, final, decay = forward_states(
        pre, halo, taps, head, e3, heads, width
    )
    carry = shifted_by(final, "col", 1)
    z = product(normed, gate_full)

    position = lax.axis_index("col") * positions + jnp.arange(positions)
    valid = (position < lengths[0]).astype(F32)[:, None]
    dmix = (cot.astype(F32) * valid).astype(BF16)
    dyn = product(dmix, output_full)
    y, enter, sums = forward_outputs(xbc, dt, state, carry, decay, z, dyn, chan, e3, heads, width)
    sums = sum_over(sums, "ta")
    yn, dssd, dz, gain_part, dstate, dfinal, fade = backward_states(
        xbc, dt, y, z, dyn, sums, chan, e3, heads, width, total_inner
    )
    dcarry = shifted_by(dfinal, "col", -1)

    mixed = with_layout_constraint(
        against(output_full, yn).astype(BF16), Layout(major_to_minor=(0, 1))
    )
    mixed = lax.psum_scatter(mixed, "ta", scatter_dimension=0, tiled=True)
    quarter = mixed.shape[0]
    own = lax.dynamic_slice_in_dim(h, lax.axis_index("ta") * quarter, quarter, 1).astype(F32)
    block_out = (own + mixed.T.astype(F32) * valid).astype(BF16)

    dpre, tail, _, rim, conv_part, head_part, skip_part = backward_inputs(
        xbc, xp, slope, dt, y, dssd, enter, dstate, dcarry, fade, jnp.zeros((8, conv), F32),
        halo, taps, head, chan, e3, heads, width, 0, positions // TB,
    )
    tail = (tail + shifted_by(rim, "col", -1)).astype(BF16)
    dpre = lax.dynamic_update_slice(dpre, tail, (positions - 8, 0))
    partial = (against(dz, gate_full) + against(dpre, packed_full)).astype(BF16)

    chunks = 4
    count = lax.axis_size("ta")
    gain_rows = jnp.broadcast_to(gain, (8, model))
    hidden_grad, arrived = None, []
    for tick in range(chunks + count - 2):
        arrived.append(
            chain_sum_step(
                partial, "ta", tick, chunks, arrived[-1] if arrived else None,
                mixed if tick == 1 else None,
            )
        )
        at = tick - count + 2
        if at >= 0:
            came = arrived[at : at + count - 1]
            hidden_grad = finish(
                at, chunks, partial, h, cot, gain_rows, [v[0] for v in came],
                [v[1] for v in came], hidden_grad,
            )

    def scattered(value):
        return lax.psum_scatter(
            value.astype(BF16), ("af", "col"), scatter_dimension=0, tiled=True
        ).astype(F32)

    output_grad = outer(dmix, yn)
    gate_grad = outer(normed, dz)
    gate_grad = scattered(after(gate_grad.astype(BF16), mixed))
    output_grad = scattered(after(output_grad.astype(BF16), gate_grad))
    packed_grad = outer(normed, dpre).astype(BF16)
    packed_grad = scatter_rows(packed_grad)

    input_grad = packed_grad[:, :width]
    state_grad = packed_grad[:, width:conv]
    step_grad = packed_grad[:, conv : conv + heads]
    rows_dot = (
        jnp.sum(gate_grad * gate_proj.astype(F32), axis=1)
        + jnp.sum(input_grad * input_proj.astype(F32), axis=1)
        + jnp.sum(state_grad * state_proj.astype(F32), axis=1)
        + jnp.sum(step_grad * step_proj.astype(F32), axis=1)
    )

    conv_sums = jnp.sum(conv_part.reshape(5, 8, conv), axis=1)
    head_sums = jnp.sum(head_part.reshape(2, 8, LANES), axis=1)
    small = jnp.concatenate(
        [
            jnp.pad(conv_sums, ((0, 0), (0, LANES * 2))),
            jnp.concatenate(
                [
                    jnp.sum(gain_part, axis=0), jnp.zeros((both,), F32), head_sums[0], head_sums[1],
                ]
            )[None, :],
            jnp.pad(jnp.sum(skip_part, axis=0), (0, both + 2 * LANES))[None, :],
            jnp.zeros((1, conv + 2 * LANES), F32),
        ],
        axis=0,
    )
    small = sum_over(sum_over(small, "col"), "af")
    gains = jnp.pad(rows_dot, (0, -local_rows % both)).reshape(-1, both)
    third = jnp.concatenate(
        [
            state_grad, small[:, width:conv], gains,
            jnp.zeros((-gains.shape[0] % 8, both), F32),
        ],
        axis=0,
    )
    third = sum_over(third, "ta")
    state_grad = third[:local_rows]
    state_small = third[local_rows:]
    gains = third[local_rows + 8 : local_rows + 8 + gains.shape[0]].reshape(-1)
    norm_gain_grad = gains[:local_rows] / norm_gain.astype(F32)
    skip_grad = jnp.sum(small[6, :width].reshape(heads, width // heads), axis=1)
    return (
        block_out[None],
        hidden_grad[None],
        norm_gain_grad,
        gate_grad,
        input_grad,
        state_grad,
        step_grad,
        small[0:4, :width],
        small[4, :width],
        state_small[0:4],
        state_small[4],
        small[5, conv : conv + heads],
        rate * small[5, conv + LANES : conv + LANES + heads],
        skip_grad,
        small[5, :width],
        output_grad,
    )


def solution(mesh):
    return mapped(mesh)


def mapped(mesh):
    return jax.shard_map(
        program,
        mesh=mesh,
        in_specs=(
            P("af", "col", None),
            P("af"),
            P(("af", "col")),
            P(("af", "col"), "ta"),
            P(("af", "col"), "ta"),
            P(("af", "col"), None),
            P(("af", "col"), "ta"),
            P(None, "ta"),
            P("ta"),
            P(),
            P(),
            P("ta"),
            P("ta"),
            P("ta"),
            P("ta"),
            P(("af", "col"), "ta"),
            P("af", "col", None),
        ),
        out_specs=(
            P("af", "col", "ta"),
            P("af", "col", None),
            P(("af", "col")),
            P(("af", "col"), "ta"),
            P(("af", "col"), "ta"),
            P(("af", "col"), None),
            P(("af", "col"), "ta"),
            P(None, "ta"),
            P("ta"),
            P(),
            P(),
            P("ta"),
            P("ta"),
            P("ta"),
            P("ta"),
            P(("af", "col"), "ta"),
        ),
        check_vma=False,
    )
```
